256 devices in a mesh: seq: 32 (over z, y_lo, core), tp: 8 (over x, y_hi).
Axes of the slice: x: 4, y: 4 (y_hi: 2, y_lo: 2; y = y_hi * 2 + y_lo), z: 8, core: 2. Of those that a mesh axis runs over, the one named last changes fastest.
Arguments:
- grad_out: bfloat16 [8192, 14336], P('seq', 'tp'), may hold values from -6 to 6
- weight: bfloat16 [4096, 14336], P('seq', 'tp'), may hold values from -0.046875 to 0.046875
- saved: bfloat16 [8192, 512], P('seq'), may hold values from -0.125 to 0.125
- first_moment: float32 [512, 14336], P('seq', 'tp'), may hold values from -6 to 6
- second_moment: float32 [512, 14336], P('seq', 'tp'), may hold values from 0.05 to 2
- basis: bfloat16 [4096, 512], P('seq'), may hold values from -0.0625 to 0.0625
- new_basis: bfloat16 [4096, 512], P('seq'), may hold values from -0.09375 to 0.09375
Outputs:
- grad_input: float32 [8192, 4096], P('seq', 'tp')
- first_new: float32 [512, 14336], P('seq', 'tp')
- second_new: float32 [512, 14336], P('seq', 'tp')
- update: float32 [512, 14336], P('seq', 'tp')
The draws below stay inside these ranges and needn't reach their ends.
All inputs are finite; a program needn't handle non-finite values.
Results may differ from the reference program's by a relative error of at most 0.0003.
Values may be sent and summed in bfloat16 or wider, within the bound.
A program may use at most 128 MiB of HBM per device.

```python
import math
import jax
import jax.numpy as jnp
from jax import lax

D = 4096
F = 14336
R = 512
TOKENS = 8192


def shared_bases(key):
    first = jax.random.truncated_normal(jax.random.fold_in(key, 11), -4.0, 4.0, (D, R), jnp.float32)
    second = jax.random.truncated_normal(jax.random.fold_in(key, 12), -4.0, 4.0, (D, R), jnp.float32)
    factor = D ** (-0.5)
    return (first * factor, (0.8 * first + 0.6 * second) * factor)


def draw_basis(key, part):
    return shared_bases(key)[0].astype(jnp.bfloat16)


def draw_new_basis(key, part):
    return shared_bases(key)[1].astype(jnp.bfloat16)


def spiked(array, own_key, source, target, blocks, factor):
    def block_of(position):
        return (jnp.arange(array.shape[position]) // (array.shape[position] // blocks)).reshape((-1,) + (1,) * (array.ndim - 1 - position))

    first = jax.random.permutation(own_key, blocks)[block_of(target)]
    other_side = (block_of(target) + blocks // 2) % blocks
    return jnp.where((block_of(source) == first) | (block_of(source) == other_side), factor * array, array)


def block_scale(key, extent, pieces, low, largest):
    loudness, own = 1.0, jax.random.fold_in(key, 6)
    for dim, parts in pieces:
        heights = jnp.exp(jax.random.uniform(jax.random.fold_in(own, dim), (parts,), jnp.float32, low / len(pieces), largest / len(pieces)))
        loudness = loudness * jnp.repeat(heights, extent[dim] // parts).reshape([-1 if axis == dim else 1 for axis in range(len(extent))])
    return loudness


def bell_draw(own_key, shape, scale, bound, split=(), kind=jnp.bfloat16):
    level = block_scale(own_key, shape, split, -0.22, 0.18) if split else 1.0
    values = jax.random.normal(own_key, shape, jnp.float32) * scale * level
    return jnp.minimum(jnp.maximum(values, -bound), bound).astype(kind)


def bell_draw_with(own_key, dims, scale, reach, pieces, heavy, held_as=jnp.bfloat16):
    array = scale * jax.random.normal(own_key, dims, jnp.float32)
    if pieces:
        array = array * block_scale(own_key, dims, pieces, -0.22, 0.18)
    return jnp.clip(spiked(array, jax.random.fold_in(own_key, 3), *heavy), -reach, reach).astype(held_as)


def setup_inputs(seed: int = 0) -> dict:
    key_of = jax.random.split(jax.random.key(seed), 8)
    grad_out = bell_draw(key_of[0], (TOKENS, F), 1.0, 6.0, ((0, 32), (1, 8)))
    weight = bell_draw(key_of[1], (D, F), F ** -0.5, 0.046875, ((0, 32), (1, 8)))
    saved = bell_draw_with(key_of[2], (TOKENS, R), TOKENS ** -0.5, 0.125, ((0, 32),), (0, 1, 32, 2.75))
    first_moment = bell_draw(key_of[3], (R, F), 1.0, 6.0, ((0, 32), (1, 8)), jnp.float32)
    second_moment = jnp.clip(jnp.exp(math.log(2.0) - 3.6888794 * jax.random.uniform(key_of[4], (R, F), jnp.float32) ** block_scale(key_of[4], (R, F), ((0, 32), (1, 8)), -0.2, 0.2)), 0.05, 2.0)
    basis = draw_basis(jax.random.fold_in(key_of[7], 71), 0)
    new_basis = draw_new_basis(jax.random.fold_in(key_of[7], 71), 0)
    return dict(grad_out=grad_out, weight=weight, saved=saved, first_moment=first_moment, second_moment=second_moment, basis=basis, new_basis=new_basis)


def reference(grad_out, weight, saved, first_moment, second_moment, basis, new_basis):
    grad_input = lax.dot_general(grad_out, weight, (((1,), (1,)), ((), ())), preferred_element_type=jnp.float32)
    gradient = lax.dot_general(saved, grad_out, (((0,), (0,)), ((), ())), preferred_element_type=jnp.float32)
    intersection = lax.dot_general(new_basis, basis, (((0,), (0,)), ((), ())), preferred_element_type=jnp.float32)
    first_rot = jnp.dot(intersection, first_moment, precision=lax.Precision.HIGHEST, preferred_element_type=jnp.float32)
    second_rot = jnp.dot(intersection * intersection, second_moment, precision=lax.Precision.HIGHEST, preferred_element_type=jnp.float32)
    first_new = 0.9 * first_rot + 0.1 * gradient
    second_new = 0.95 * second_rot + 0.05 * gradient * gradient
    update = first_new / (jnp.sqrt(second_new) + 1e-08)
    return (grad_input, first_new, second_new, update)
```

```python
import jax
import jax.numpy as jnp
from jax import lax
from jax.experimental import pallas as pl
from jax.experimental.pallas import tpu as pltpu
from jax.sharding import PartitionSpec as P

MESH = pl.DeviceIdType.MESH
F32 = jnp.float32
BF16 = jnp.bfloat16
NZ = 8
TOK = 256
COLS = 1792
HALF = COLS // 2
RANK = 512
ROWS = 16
DROWS = 128
WIDE = COLS + RANK


def rem(a, b):
    return lax.rem(a, jnp.int32(b))


def div(a, b):
    return lax.div(a, jnp.int32(b))


def kernel(
    go, w, sv, fm, sm, ba, nb,
    o_gi, o_f, o_s, o_u,
    Gs, Ws, Pp, Xh, X0, Ff, St, Sq, Nt, Nq, Bs, Ms, Z, ZR, I64, RT, Rr,
    loc, g_s, g_r, k_s, k_r, w_s, w_r, m_s, m_r, z_s, z_r, xa_s, xb_s, h_r, x0_r, f_r,
):
    s = lax.axis_index("seq")
    t = lax.axis_index("tp")
    z, k = div(s, 4), rem(s, 4)
    yl, c = div(k, 2), rem(k, 2)
    x, yh = div(t, 2), rem(t, 2)

    def mate(rel):
        if isinstance(rel, int):
            a, b = rel // 2, rel % 2
        else:
            a, b = div(rel, 2), rem(rel, 2)
        return rem(yl + a, 2) * 2 + rem(c + b, 2)

    def group_dev(rel):
        return (z * 4 + mate(rel), t)

    zl = (rem(z + NZ - 1, NZ) * 4 + k, t)
    zr = (rem(z + 1, NZ) * 4 + k, t)
    xl = (s, rem(x + 3, 4) * 2 + yh)
    xr = (s, rem(x + 1, 4) * 2 + yh)

    barrier = pltpu.get_barrier_semaphore()
    partners = [group_dev(1), group_dev(2), group_dev(3), zl, zr, xl, xr]
    partners += [(z * 4 + mate(r), x * 2 + (1 - yh)) for r in range(4)]
    for dev in partners:
        pl.semaphore_signal(barrier, inc=1, device_id=dev, device_id_type=MESH)
    pl.semaphore_wait(barrier, len(partners))

    def remote(src, dst, ss, rs, dev):
        return pltpu.make_async_remote_copy(
            src_ref=src, dst_ref=dst, send_sem=ss, recv_sem=rs, device_id=dev, device_id_type=MESH
        )

    def zslot(d):
        return 0 if d == 0 else (2 * d - 1 if d > 0 else -2 * d)

    def w_copy(way, j, h):
        sign = 1 if way == 0 else -1
        dst = 7 if j == 4 else zslot(sign * j)
        rows = pl.ds(h * 64, 64)
        src = w.at[rows] if j == 1 else Ws.at[zslot(sign * (j - 1)), rows]
        return remote(src, Ws.at[dst, rows], w_s.at[way, j - 1, h], w_r.at[way, j - 1, h],
                      zl if way == 0 else zr)

    def m_copy(way, j, h, arriving=False):
        dist = j if arriving else j - 1
        blk = rem(z + dist, NZ) if way == 0 else rem(z + NZ - dist, NZ)
        rows = pl.ds(pl.multiple_of(blk * 64 + h * 32, 32), 32)
        return remote(Ms.at[rows], Ms.at[rows], m_s.at[way, j - 1, h], m_r.at[way, j - 1, h],
                      zl if way == 0 else zr)

    def g_copy(rel, h):
        rows = pl.ds(h * 128, 128)
        if rel == 3:
            return remote(Gs.at[2, rows], Gs.at[3, rows], g_s.at[2, h], g_r.at[2, h], group_dev(1))
        return remote(go.at[rows], Gs.at[rel, rows], g_s.at[rel - 1, h], g_r.at[rel - 1, h], group_dev(rel))

    def b_copy(rel):
        if rel == 3:
            return remote(Bs.at[2], Bs.at[3], k_s.at[0, 2], k_r.at[0, 2], group_dev(1))
        return remote(ba, Bs.at[rel], k_s.at[0, rel - 1], k_r.at[0, rel - 1], group_dev(rel))

    def sq_copy(rel):
        return remote(St.at[:, mate(rel)], Sq.at[rel], k_s.at[1, rel - 1], k_r.at[1, rel - 1], group_dev(rel))

    def nq_copy(rel):
        return remote(Nt.at[:, mate(rel)], Nq.at[rel], k_s.at[2, rel - 1], k_r.at[2, rel - 1], group_dev(rel))

    own_rows = pl.ds(pl.multiple_of(z * 64 + k * 16, 16), 16)

    def ma_copy(rel, moment):
        half = rem(yl + rel // 2, 2)
        cols = pl.ds(pl.multiple_of(half * HALF, 128), HALF)
        return remote(moment.at[:, cols], Ms.at[own_rows], k_s.at[3, rel - 1], k_r.at[3, rel - 1], group_dev(rel))

    def i_copy(rel):
        return remote(Z.at[z, :, pl.ds(COLS, RANK)], I64.at[k], k_s.at[4, rel - 1], k_r.at[4, rel - 1], group_dev(rel))

    def r_copy(rel):
        rows = pl.ds(pl.multiple_of(mate(rel) * 16, 16), 16)
        return remote(RT.at[rows], Rr.at[c, yl], k_s.at[5, rel - 1], k_r.at[5, rel - 1], group_dev(rel))

    def z_cols(way, j):
        if j == 0:
            return pl.ds(0, WIDE // 2) if way == 1 else pl.ds(WIDE // 2, WIDE // 2)
        return pl.ds(0, WIDE)

    def z_block(way, j):
        dist = 4 - j
        return rem(z + dist, NZ) if way == 1 else rem(z + NZ - dist, NZ)

    def z_copy(way, j):
        cols = z_cols(way, j)
        return remote(Z.at[z_block(way, j), :, cols], ZR.at[way, j, :, cols], z_s.at[way, j], z_r.at[way, j],
                      zl if way == 0 else zr)

    def cp_a(di, rel):
        return remote(Pp.at[di, rel, pl.ds(0, 128)], Xh.at[di, rel], xa_s.at[di, rel], h_r.at[di, rel], xl)

    def cp_b(di, rel):
        return remote(Pp.at[di, rel, pl.ds(128, 128)], Xh.at[di, rel], xb_s.at[di, rel], h_r.at[di, rel], xr)

    def cp_full(side, di, rel):
        return remote(Pp.at[di, rel], X0.at[side, di, rel], xa_s.at[di, rel], x0_r.at[side, di, rel],
                      xl if side == 0 else xr)

    def cp_f(di, rel, zt, ry):
        return remote(Pp.at[di, rel], Ff.at[ry, rel], xa_s.at[di, rel], f_r.at[ry, rel], (z * 4 + mate(rel), zt))

    def where_to(di):
        mag = div(di + 1, 2)
        d = mag * (2 * rem(di, 2) - 1)
        zt = rem(z + d + NZ, NZ)
        role = rem(x - div(zt, 2) + 4, 4)
        return zt, role

    def stage1(di, rel):
        Pp[di, rel] = lax.dot_general(Gs[rel], Ws[di], (((1,), (1,)), ((), ())), preferred_element_type=F32)
        _, role = where_to(di)

        @pl.when(role == 2)
        def _():
            cp_a(di, rel).start()
            cp_b(di, rel).start()

    def stage2(di, rel):
        _, role = where_to(di)

        @pl.when(role == 1)
        def _():
            cp_a(di, rel).wait_recv()
            Pp[di, rel, pl.ds(0, 128)] = Pp[di, rel, pl.ds(0, 128)] + Xh[di, rel]
            cp_full(0, di, rel).start()

        @pl.when(role == 3)
        def _():
            cp_b(di, rel).wait_recv()
            Pp[di, rel, pl.ds(128, 128)] = Pp[di, rel, pl.ds(128, 128)] + Xh[di, rel]
            cp_full(1, di, rel).start()

    def stage3(di, rel):
        zt, role = where_to(di)

        @pl.when(role == 0)
        def _():
            cp_full(0, di, rel).wait_recv()
            cp_full(1, di, rel).wait_recv()
            total = Pp[di, rel] + X0[0, di, rel] + X0[1, di, rel]
            ry = rem(rem(zt, 2) + yh, 2)
            local = ry + rel == 0

            @pl.when(local)
            def _():
                Ff[0, 0] = total

            @pl.when(jnp.logical_not(local))
            def _():
                Pp[di, rel] = total
                cp_f(di, rel, zt, ry).start()

    def drain(di, rel):
        zt, role = where_to(di)
        ry = rem(rem(zt, 2) + yh, 2)

        @pl.when(role == 2)
        def _():
            cp_a(di, rel).wait_send()
            cp_b(di, rel).wait_send()

        @pl.when(rem(role, 2) == 1)
        def _():
            cp_full(0, di, rel).wait_send()

        @pl.when(jnp.logical_and(role == 0, ry + rel > 0))
        def _():
            cp_f(di, rel, zt, ry).wait_send()

    def run(stage, group):
        d0, dn, r0, rn = group

        def step(i, carry):
            stage(d0 + div(i, rn), r0 + rem(i, rn))
            return carry

        lax.fori_loop(jnp.int32(0), jnp.int32(dn * rn), step, jnp.int32(0))

    A0, A1 = (0, 1, 0, 1), (0, 1, 1, 1)
    A, B, C, D, E, F = (0, 1, 0, 2), (1, 2, 0, 2), (3, 2, 0, 2), (0, 5, 2, 2), (5, 2, 0, 4), (7, 1, 0, 4)

    FIRST = {0: 0, 1: 1}

    def w_hop(j, second):
        for way in (0, 1):
            h = 1 - FIRST[way] if second else FIRST[way]
            if j == 4 and second:
                continue
            w_copy(way, j, h).wait_recv()
            if j < 3 or (j == 3 and not second):
                w_copy(way, j + 1, h).start()

    def m_hop(j, second):
        for way in (0, 1):
            h = 1 - FIRST[way] if second else FIRST[way]
            if j == 4 and second:
                continue
            m_copy(way, j, h, arriving=True).wait_recv()
            if j < 3 or (j == 3 and not second):
                m_copy(way, j + 1, h).start()

    def z_step(j):
        for way in (0, 1):
            if j > 0:
                z_copy(way, j - 1).wait_recv()
                cols = z_cols(way, j - 1)
                blk = z_block(way, j)
                Z[blk, :, cols] = Z[blk, :, cols] + ZR[way, j - 1, :, cols]
            if j < 4:
                z_copy(way, j).start()

    for second in (False, True):
        for way in (0, 1):
            w_copy(way, 1, 1 - FIRST[way] if second else FIRST[way]).start()
    for h in (0, 1):
        g_copy(1, h).start()
    for h in (0, 1):
        g_copy(2, h).start()
    own_g = pltpu.make_async_copy(go, Gs.at[0], loc.at[0])
    own_w = pltpu.make_async_copy(w, Ws.at[0], loc.at[1])
    own_b = pltpu.make_async_copy(ba, Bs.at[0], loc.at[2])
    for cp in (own_g, own_w, own_b):
        cp.start()
    own_cols = pl.ds(pl.multiple_of(yl * HALF, 128), HALF)

    @pl.when(c == 0)
    def _():
        pltpu.make_async_copy(fm.at[:, own_cols], Ms.at[own_rows], loc.at[3]).start()

    @pl.when(c == 1)
    def _():
        pltpu.make_async_copy(sm.at[:, own_cols], Ms.at[own_rows], loc.at[3]).start()

    St[...] = jnp.transpose(sv[...].astype(F32)).astype(BF16).reshape(8, 4, 16, TOK)
    Nt[...] = jnp.transpose(nb[...].astype(F32)).astype(BF16).reshape(8, 4, 16, DROWS)
    Sq[0] = St[:, k]
    Nq[0] = Nt[:, k]
    for rel in (1, 2, 3):
        sq_copy(rel).start()
    for rel in (1, 2, 3):
        nq_copy(rel).start()
    for rel in (1, 2):
        b_copy(rel).start()
    for rel in (1, 2, 3):
        other = rem(c + rel % 2, 2)

        @pl.when(other == 0)
        def _(rel=rel):
            ma_copy(rel, fm).start()

        @pl.when(other == 1)
        def _(rel=rel):
            ma_copy(rel, sm).start()

    own_g.wait()
    own_w.wait()
    run(stage1, A0)
    for h in (0, 1):
        g_copy(1, h).wait_recv()
    run(stage1, A1)
    w_hop(1, False)
    w_hop(1, True)
    g_copy(2, 0).wait_recv()
    g_copy(3, 0).start()
    run(stage1, B)
    run(stage2, A)
    w_hop(2, False)
    run(stage3, A)
    w_hop(2, True)
    run(stage1, C)
    run(stage2, B)
    g_copy(2, 1).wait_recv()
    g_copy(3, 1).start()
    b_copy(2).wait_recv()
    b_copy(3).start()
    g_copy(3, 0).wait_recv()
    g_copy(3, 1).wait_recv()
    run(stage1, D)

    for rel in (1, 2, 3):
        sq_copy(rel).wait_recv()

    def grad_tile(i, carry):
        cols = pl.ds(pl.multiple_of(i * 256, 256), 256)
        acc = jnp.zeros((DROWS, 256), F32)
        for rel in range(4):
            acc += jnp.dot(Sq[rel].reshape(DROWS, TOK), Gs[rel, :, cols], preferred_element_type=F32)
        Z[:, :, cols] = acc.reshape(8, 16, 256)
        return carry

    lax.fori_loop(jnp.int32(0), jnp.int32(COLS // 256), grad_tile, jnp.int32(0))
    own_b.wait()
    b_copy(1).wait_recv()
    b_copy(3).wait_recv()
    for rel in (1, 2, 3):
        nq_copy(rel).wait_recv()
    inter = jnp.zeros((DROWS, RANK), F32)
    for rel in range(4):
        inter += jnp.dot(Nq[rel].reshape(DROWS, DROWS), Bs[rel], preferred_element_type=F32)
    Z[:, :, pl.ds(COLS, RANK)] = inter.reshape(8, 16, RANK)

    w_hop(3, False)
    z_step(0)
    run(stage2, C)
    run(stage3, B)
    w_hop(3, True)
    for rel in (1, 2, 3):
        ma_copy(rel, fm).wait_recv()
    pltpu.make_async_copy(fm.at[:, own_cols], Ms.at[own_rows], loc.at[3]).wait()
    for second in (False, True):
        for way in (0, 1):
            m_copy(way, 1, 1 - FIRST[way] if second else FIRST[way]).start()
    run(stage1, E)
    z_step(1)
    run(stage2, D)
    run(stage3, C)
    w_hop(4, False)
    run(stage1, F)
    m_hop(1, False)
    run(stage2, E)
    m_hop(1, True)
    z_step(2)
    run(stage3, D)
    m_hop(2, False)
    run(stage2, F)
    z_step(3)
    m_hop(2, True)
    run(stage3, E)
    m_hop(3, False)
    z_step(4)
    I64[k] = Z[z, :, pl.ds(COLS, RANK)]
    for rel in (1, 2, 3):
        i_copy(rel).start()
    run(stage3, F)
    m_hop(3, True)
    for rel in (1, 2, 3):
        i_copy(rel).wait_recv()
    m_hop(4, False)

    coef = I64[...].reshape(64, RANK)
    coef = jnp.where(c == 0, coef, coef * coef)
    RT[...] = jnp.dot(coef, Ms[...], precision=lax.Precision.HIGHEST, preferred_element_type=F32)
    for rel in (1, 2, 3):
        r_copy(rel).start()
    Rr[c, yl] = RT[pl.ds(pl.multiple_of(k * 16, 16), 16)]

    for ry in (0, 1):
        for rel in range(4):
            if ry + rel > 0:
                remote(Ff.at[ry, rel], Ff.at[ry, rel], f_r.at[ry, rel], f_r.at[ry, rel], xl).wait_recv()
    for rel in range(4):
        o_gi[:, pl.ds(pl.multiple_of(mate(rel) * 128, 128), 128)] = Ff[0, rel] + Ff[1, rel]

    for rel in (1, 2, 3):
        r_copy(rel).wait_recv()
    for h in (0, 1):
        cols = pl.ds(h * HALF, HALF)
        grad = Z[z, :, cols]
        first = 0.9 * Rr[0, h] + 0.1 * grad
        second = 0.95 * Rr[1, h] + 0.05 * grad * grad
        o_f[:, cols] = first
        o_s[:, cols] = second
        o_u[:, cols] = first / (jnp.sqrt(second) + 1e-8)

    for j in (1, 2, 3, 4):
        for way in (0, 1):
            for h in (0, 1):
                if j < 4 or h == FIRST[way]:
                    w_copy(way, j, h).wait_send()
                    m_copy(way, j, h).wait_send()
    for h in (0, 1):
        for rel in (1, 2, 3):
            g_copy(rel, h).wait_send()
    for rel in (1, 2, 3):
        b_copy(rel).wait_send()
        sq_copy(rel).wait_send()
        nq_copy(rel).wait_send()
        ma_copy(rel, fm).wait_send()
        i_copy(rel).wait_send()
        r_copy(rel).wait_send()
    for j in range(4):
        for way in (0, 1):
            z_copy(way, j).wait_send()
    run(drain, (0, 8, 0, 4))


def per_device(grad_out, weight, saved, first_moment, second_moment, basis, new_basis):
    vmem = pl.BlockSpec(memory_space=pltpu.VMEM)
    dma = pltpu.SemaphoreType.DMA
    rank = jax.ShapeDtypeStruct((ROWS, COLS), F32)
    return pl.pallas_call(
        kernel,
        out_shape=(jax.ShapeDtypeStruct((TOK, RANK), F32), rank, rank, rank),
        in_specs=[vmem] * 7,
        out_specs=(vmem,) * 4,
        scratch_shapes=[
            pltpu.VMEM((4, TOK, COLS), BF16),
            pltpu.VMEM((8, DROWS, COLS), BF16),
            pltpu.VMEM((8, 4, TOK, DROWS), F32),
            pltpu.VMEM((8, 4, DROWS, DROWS), F32),
            pltpu.VMEM((2, 8, 4, TOK, DROWS), F32),
            pltpu.VMEM((2, 4, TOK, DROWS), F32),
            pltpu.VMEM((8, 4, 16, TOK), BF16),
            pltpu.VMEM((4, 8, 16, TOK), BF16),
            pltpu.VMEM((8, 4, 16, DROWS), BF16),
            pltpu.VMEM((4, 8, 16, DROWS), BF16),
            pltpu.VMEM((4, DROWS, RANK), BF16),
            pltpu.VMEM((RANK, HALF), F32),
            pltpu.VMEM((8, 16, WIDE), F32),
            pltpu.VMEM((2, 4, 16, WIDE), F32),
            pltpu.VMEM((4, 16, RANK), F32),
            pltpu.VMEM((64, HALF), F32),
            pltpu.VMEM((2, 2, 16, HALF), F32),
            dma((4,)),
            dma((3, 2)),
            dma((3, 2)),
            dma((6, 3)),
            dma((6, 3)),
            dma((2, 4, 2)),
            dma((2, 4, 2)),
            dma((2, 4, 2)),
            dma((2, 4, 2)),
            dma((2, 4)),
            dma((2, 4)),
            dma((8, 4)),
            dma((8, 4)),
            dma((8, 4)),
            dma((2, 8, 4)),
            dma((2, 4)),
        ],
        compiler_params=pltpu.CompilerParams(
            collective_id=0, has_side_effects=True, vmem_limit_bytes=56 * 1024 * 1024
        ),
    )(grad_out, weight, saved, first_moment, second_moment, basis, new_basis)


def solution(mesh):
    return jax.shard_map(
        per_device,
        mesh=mesh,
        in_specs=(
            P("seq", "tp"),
            P("seq", "tp"),
            P("seq", None),
            P("seq", "tp"),
            P("seq", "tp"),
            P("seq", None),
            P("seq", None),
        ),
        out_specs=(P("seq", "tp"), P("seq", "tp"), P("seq", "tp"), P("seq", "tp")),
        check_vma=False,
    )
```

```python
import jax
import jax.numpy as jnp
from jax import lax
from jax.experimental import pallas as pl
from jax.experimental.pallas import tpu as pltpu
from jax.sharding import PartitionSpec as P

MESH = pl.DeviceIdType.MESH
F32 = jnp.float32
BF16 = jnp.bfloat16
NZ = 8
TOK = 256
COLS = 1792
HALF = COLS // 2
RANK = 512
ROWS = 16
DROWS = 128


def rem(a, b):
    return lax.rem(a, jnp.int32(b))


def div(a, b):
    return lax.div(a, jnp.int32(b))


def kernel(
    go, w, sv_h, fm, sm, ba, nb_h,
    o_gi, o_f, o_s, o_u,
    sv, nb, Gs, Ws, Pp, Xa, Xb, Ff, St, Sq, Nt, Nq, Bs, Ms, Z, ZR, Y, YR, I64, RT, Rr, gi_v, f_v, s_v, u_v,
    loc, g_s, g_r, k_s, k_r, w_s, w_r, m_s, m_r, z_s, z_r, y_s, y_r, xa_s, xb_s, xa_r, xb_r, f_s, f_r,
):
    s = lax.axis_index("seq")
    t = lax.axis_index("tp")
    z, k = div(s, 4), rem(s, 4)
    yl, c = div(k, 2), rem(k, 2)
    x, yh = div(t, 2), rem(t, 2)

    def mate(rel):
        if isinstance(rel, int):
            a, b = rel // 2, rel % 2
        else:
            a, b = div(rel, 2), rem(rel, 2)
        return rem(yl + a, 2) * 2 + rem(c + b, 2)

    def group_dev(rel):
        return (z * 4 + mate(rel), t)

    zl = (rem(z + NZ - 1, NZ) * 4 + k, t)
    zr = (rem(z + 1, NZ) * 4 + k, t)
    xl = (s, rem(x + 3, 4) * 2 + yh)
    xr = (s, rem(x + 1, 4) * 2 + yh)

    own_rows = pl.ds(pl.multiple_of(z * 64 + k * 16, 16), 16)
    own_cols = pl.ds(pl.multiple_of(yl * HALF, 128), HALF)
    own_g = pltpu.make_async_copy(go, Gs.at[0], loc.at[0])
    own_w = pltpu.make_async_copy(w, Ws.at[0], loc.at[1])
    own_b = pltpu.make_async_copy(ba, Bs.at[0], loc.at[2])
    own_sv = pltpu.make_async_copy(sv_h, sv, loc.at[4])
    own_nb = pltpu.make_async_copy(nb_h, nb, loc.at[5])
    for cp in (own_g, own_w, own_sv, own_nb, own_b):
        cp.start()

    @pl.when(c == 0)
    def _():
        pltpu.make_async_copy(fm.at[:, own_cols], Ms.at[own_rows], loc.at[3]).start()

    @pl.when(c == 1)
    def _():
        pltpu.make_async_copy(sm.at[:, own_cols], Ms.at[own_rows], loc.at[3]).start()

    barrier = pltpu.get_barrier_semaphore()
    partners = [group_dev(1), group_dev(2), group_dev(3), zl, zr, xl, xr]
    partners += [(z * 4 + mate(r), x * 2 + (1 - yh)) for r in range(4)]
    for dev in partners:
        pl.semaphore_signal(barrier, inc=1, device_id=dev, device_id_type=MESH)
    pl.semaphore_wait(barrier, len(partners))

    def remote(src, dst, ss, rs, dev):
        return pltpu.make_async_remote_copy(
            src_ref=src, dst_ref=dst, send_sem=ss, recv_sem=rs, device_id=dev, device_id_type=MESH
        )

    def zslot(d):
        return 0 if d == 0 else (2 * d - 1 if d > 0 else -2 * d)

    def w_copy(way, j, h):
        sign = 1 if way == 0 else -1
        dst = 7 if j == 4 else zslot(sign * j)
        rows = pl.ds(h * 64, 64)
        src = w.at[rows] if j == 1 else Ws.at[zslot(sign * (j - 1)), rows]
        return remote(src, Ws.at[dst, rows], w_s.at[way, j - 1, h], w_r.at[way, j - 1, h],
                      zl if way == 0 else zr)

    def m_copy(way, j, h, arriving=False):
        dist = j if arriving else j - 1
        blk = rem(z + dist, NZ) if way == 0 else rem(z + NZ - dist, NZ)
        rows = pl.ds(pl.multiple_of(blk * 64 + h * 32, 32), 32)
        return remote(Ms.at[rows], Ms.at[rows], m_s.at[way, j - 1, h], m_r.at[way, j - 1, h],
                      zl if way == 0 else zr)

    def g_copy(rel, h):
        rows = pl.ds(h * 128, 128)
        if rel == 3:
            return remote(Gs.at[2, rows], Gs.at[3, rows], g_s.at[2, h], g_r.at[2, h], group_dev(1))
        return remote(go.at[rows], Gs.at[rel, rows], g_s.at[rel - 1, h], g_r.at[rel - 1, h], group_dev(rel))

    def b_copy(rel):
        if rel == 3:
            return remote(Bs.at[2], Bs.at[3], k_s.at[0, 2], k_r.at[0, 2], group_dev(1))
        return remote(ba, Bs.at[rel], k_s.at[0, rel - 1], k_r.at[0, rel - 1], group_dev(rel))

    def sq_copy(rel):
        return remote(St.at[:, mate(rel)], Sq.at[rel], k_s.at[1, rel - 1], k_r.at[1, rel - 1], group_dev(rel))

    def nq_copy(rel):
        return remote(Nt.at[:, mate(rel)], Nq.at[rel], k_s.at[2, rel - 1], k_r.at[2, rel - 1], group_dev(rel))

    def ma_copy(rel, moment):
        half = rem(yl + rel // 2, 2)
        cols = pl.ds(pl.multiple_of(half * HALF, 128), HALF)
        return remote(moment.at[:, cols], Ms.at[own_rows], k_s.at[3, rel - 1], k_r.at[3, rel - 1], group_dev(rel))

    def i_copy(rel):
        return remote(Y.at[z], I64.at[k], k_s.at[4, rel - 1], k_r.at[4, rel - 1], group_dev(rel))

    def r_copy(rel):
        rows = pl.ds(pl.multiple_of(mate(rel) * 16, 16), 16)
        return remote(RT.at[rows], Rr.at[c, yl], k_s.at[5, rel - 1], k_r.at[5, rel - 1], group_dev(rel))

    def z_block(way, j):
        dist = 4 - j
        return rem(z + dist, NZ) if way == 1 else rem(z + NZ - dist, NZ)

    class Tree:
        def __init__(self, own, got, width, ss, rs):
            self.own, self.got, self.width, self.ss, self.rs = own, got, width, ss, rs

        def cols(self, way, j):
            if j == 0:
                return pl.ds((1 - way) * (self.width // 2), self.width // 2)
            return pl.ds(0, self.width)

        def copy(self, way, j):
            cols = self.cols(way, j)
            return remote(self.own.at[z_block(way, j), :, cols], self.got.at[way, j, :, cols],
                          self.ss.at[way, j], self.rs.at[way, j], zl if way == 0 else zr)

        def step(self, j):
            for way in (0, 1):
                if j > 0:
                    self.copy(way, j - 1).wait_recv()
                    cols = self.cols(way, j - 1)
                    blk = z_block(way, j)
                    self.own[blk, :, cols] = self.own[blk, :, cols] + self.got[way, j - 1, :, cols]
                if j < 4:
                    self.copy(way, j).start()

    z_step = Tree(Z, ZR, COLS, z_s, z_r).step
    i_step = Tree(Y, YR, RANK, y_s, y_r).step

    def cp_a(di, rel):
        return remote(Pp.at[di, rel, pl.ds(0, 128)], Xa.at[di, rel], xa_s.at[di], xa_r.at[di, rel], xl)

    def cp_b(di, rel):
        return remote(Pp.at[di, rel, pl.ds(128, 128)], Xb.at[di, rel], xb_s.at[di], xb_r.at[di, rel], xr)

    def cp_f(di, rel, zt, ry):
        return remote(Pp.at[di, rel], Ff.at[ry, rel], f_s.at[ry, rel], f_r.at[ry, rel], (z * 4 + mate(rel), zt))

    def where_to(di):
        mag = div(di + 1, 2)
        d = mag * (2 * rem(di, 2) - 1)
        zt = rem(z + d + NZ, NZ)
        role = rem(x - div(zt, 2) + 4, 4)
        return zt, role

    def take_a(di, rel):
        cp_a(di, rel).wait_recv()
        Pp[di, rel, pl.ds(0, 128)] = Pp[di, rel, pl.ds(0, 128)] + Xa[di, rel]

    def take_b(di, rel):
        cp_b(di, rel).wait_recv()
        Pp[di, rel, pl.ds(128, 128)] = Pp[di, rel, pl.ds(128, 128)] + Xb[di, rel]

    def stage1(di, rel):
        Pp[di, rel] = lax.dot_general(Gs[rel], Ws[di], (((1,), (1,)), ((), ())), preferred_element_type=F32)
        launch(di, rel)

    def stage1_pair(dp, rel):
        di = 2 * dp - 1
        both = Ws[pl.ds(di, 2)].reshape(2 * DROWS, COLS)
        out = lax.dot_general(Gs[rel], both, (((1,), (1,)), ((), ())), preferred_element_type=F32)
        Pp[di, rel] = out[:, :DROWS]
        Pp[di + 1, rel] = out[:, DROWS:]
        launch(di, rel)
        launch(di + 1, rel)

    def launch(di, rel):
        _, role = where_to(di)

        @pl.when(role == 3)
        def _():
            cp_a(di, rel).start()

        @pl.when(role == 1)
        def _():
            cp_b(di, rel).start()

    def stage2(di, rel):
        _, role = where_to(di)

        @pl.when(role == 2)
        def _():
            take_a(di, rel)
            cp_a(di, rel).start()
            take_b(di, rel)
            cp_b(di, rel).start()

    def stage3(di, rel):
        _, role = where_to(di)

        @pl.when(role == 1)
        def _():
            take_a(di, rel)
            cp_a(di, rel).start()

        @pl.when(role == 3)
        def _():
            take_b(di, rel)
            cp_b(di, rel).start()

    def stage4(di, rel):
        zt, role = where_to(di)

        @pl.when(role == 0)
        def _():
            cp_a(di, rel).wait_recv()
            cp_b(di, rel).wait_recv()
            ry = rem(rem(zt, 2) + yh, 2)
            local = ry + rel == 0
            upper = Pp[di, rel, pl.ds(0, 128)] + Xa[di, rel]
            lower = Pp[di, rel, pl.ds(128, 128)] + Xb[di, rel]

            @pl.when(local)
            def _():
                Ff[0, 0, pl.ds(0, 128)] = upper
                Ff[0, 0, pl.ds(128, 128)] = lower

            @pl.when(jnp.logical_not(local))
            def _():
                Pp[di, rel, pl.ds(0, 128)] = upper
                Pp[di, rel, pl.ds(128, 128)] = lower
                cp_f(di, rel, zt, ry).start()

    def drain(di, unused):
        zt, role = where_to(di)
        ry = rem(rem(zt, 2) + yh, 2)

        @pl.when(role > 0)
        def _():
            upper = Pp.at[di, :, pl.ds(0, 128)]
            lower = Pp.at[di, :, pl.ds(128, 128)]
            remote(upper, upper, xa_s.at[di], xa_s.at[di], xl).wait_send()
            remote(lower, lower, xb_s.at[di], xb_s.at[di], xr).wait_send()

        @pl.when(role == 0)
        def _():
            for rel in range(4):
                if rel > 0:
                    cp_f(di, rel, zt, ry).wait_send()
                else:
                    @pl.when(ry > 0)
                    def _():
                        cp_f(di, 0, zt, ry).wait_send()

    def run(stage, group):
        d0, dn, r0, rn = group

        def step(i, carry):
            stage(d0 + div(i, rn), r0 + rem(i, rn))
            return carry

        lax.fori_loop(jnp.int32(0), jnp.int32(dn * rn), step, jnp.int32(0))

    A0, A1 = (0, 1, 0, 1), (0, 1, 1, 1)
    A, B, C, F = (0, 1, 0, 2), (1, 2, 0, 2), (3, 2, 0, 2), (7, 1, 0, 4)
    PB, PC, PD2, PD3, PE = (1, 1, 0, 2), (2, 1, 0, 2), (1, 1, 2, 2), (2, 1, 2, 2), (3, 1, 0, 4)
    D1, D2, D3 = (0, 1, 2, 2), (1, 2, 2, 2), (3, 2, 2, 2)
    E1, E2 = (5 + rem(z + 1, 2), 1, 0, 4), (5 + rem(z, 2), 1, 0, 4)

    FIRST = {0: 0, 1: 1}

    def w_hop(j, second):
        for way in (0, 1):
            h = 1 - FIRST[way] if second else FIRST[way]
            if j == 4 and second:
                continue
            w_copy(way, j, h).wait_recv()
            if j < 3 or (j == 3 and not second):
                w_copy(way, j + 1, h).start()

    def m_hop(j, second):
        for way in (0, 1):
            h = 1 - FIRST[way] if second else FIRST[way]
            if j == 4 and second:
                continue
            m_copy(way, j, h, arriving=True).wait_recv()
            if j < 3 or (j == 3 and not second):
                m_copy(way, j + 1, h).start()

    for second in (False, True):
        for way in (0, 1):
            w_copy(way, 1, 1 - FIRST[way] if second else FIRST[way]).start()
    for rel in (1, 2, 3):
        other = rem(c + rel % 2, 2)

        @pl.when(other == 0)
        def _(rel=rel):
            ma_copy(rel, fm).start()

        @pl.when(other == 1)
        def _(rel=rel):
            ma_copy(rel, sm).start()

    for h in (0, 1):
        g_copy(2, h).start()
    for h in (0, 1):
        g_copy(1, h).start()
    own_g.wait()
    own_w.wait()
    run(stage1, A0)
    for h in (0, 1):
        g_copy(1, h).wait_recv()
    run(stage1, A1)

    own_sv.wait()
    own_nb.wait()
    St[...] = jnp.transpose(sv[...].astype(F32)).astype(BF16).reshape(8, 4, 16, TOK)
    Nt[...] = jnp.transpose(nb[...].astype(F32)).astype(BF16).reshape(8, 4, 16, DROWS)
    Sq[0] = St[:, k]
    Nq[0] = Nt[:, k]
    for rel in (1, 2, 3):
        sq_copy(rel).start()
    for rel in (1, 2):
        b_copy(rel).start()
    for rel in (1, 2, 3):
        nq_copy(rel).start()
    w_hop(1, False)
    run(stage2, A)
    w_hop(1, True)
    run(stage3, A)
    g_copy(2, 0).wait_recv()
    g_copy(3, 0).start()
    run(stage1_pair, PB)
    w_hop(2, False)
    run(stage4, A)
    run(stage2, B)
    w_hop(2, True)
    run(stage1_pair, PC)
    run(stage3, B)
    g_copy(2, 1).wait_recv()
    g_copy(3, 1).start()
    g_copy(3, 0).wait_recv()
    g_copy(3, 1).wait_recv()
    run(stage1, D1)
    w_hop(3, False)
    run(stage1_pair, PD2)
    run(stage1_pair, PD3)
    run(stage2, C)
    b_copy(2).wait_recv()
    b_copy(3).start()

    for rel in (1, 2, 3):
        sq_copy(rel).wait_recv()

    def grad_tile(i, carry):
        cols = pl.ds(pl.multiple_of(i * 256, 256), 256)
        acc = jnp.zeros((DROWS, 256), F32)
        for rel in range(4):
            acc += jnp.dot(Sq[rel].reshape(DROWS, TOK), Gs[rel, :, cols], preferred_element_type=F32)
        Z[:, :, cols] = acc.reshape(8, 16, 256)
        return carry

    lax.fori_loop(jnp.int32(0), jnp.int32(COLS // 256), grad_tile, jnp.int32(0))
    own_b.wait()
    b_copy(1).wait_recv()
    b_copy(3).wait_recv()
    for rel in (1, 2, 3):
        nq_copy(rel).wait_recv()
    inter = jnp.zeros((DROWS, RANK), F32)
    for rel in range(4):
        inter += jnp.dot(Nq[rel].reshape(DROWS, DROWS), Bs[rel], preferred_element_type=F32)
    Y[...] = inter.reshape(8, 16, RANK)
    i_step(0)
    z_step(0)
    for rel in (1, 2, 3):
        ma_copy(rel, fm).wait_recv()
    pltpu.make_async_copy(fm.at[:, own_cols], Ms.at[own_rows], loc.at[3]).wait()
    for second in (False, True):
        for way in (0, 1):
            m_copy(way, 1, 1 - FIRST[way] if second else FIRST[way]).start()
    run(stage2, D1)
    run(stage4, B)
    w_hop(3, True)
    run(stage1_pair, PE)
    run(stage3, C)
    run(stage2, D2)
    run(stage3, D1)
    run(stage2, D3)
    w_hop(4, False)
    run(stage1, F)
    i_step(1)
    z_step(1)
    run(stage2, E1)
    run(stage4, C)
    run(stage3, D2)
    m_hop(1, False)
    run(stage4, D1)
    i_step(2)
    m_hop(1, True)
    run(stage2, F)
    run(stage3, D3)
    run(stage3, E1)
    z_step(2)
    run(stage2, E2)
    m_hop(2, False)
    i_step(3)
    run(stage4, D2)
    run(stage4, D3)
    m_hop(2, True)
    run(stage3, F)
    run(stage4, E1)
    i_step(4)
    I64[k] = Y[z]
    for rel in (1, 2, 3):
        i_copy(rel).start()
    run(stage3, E2)
    z_step(3)
    m_hop(3, False)
    run(stage4, F)
    m_hop(3, True)
    run(stage4, E2)
    run(drain, (0, 5, 0, 1))
    for rel in (1, 2, 3):
        i_copy(rel).wait_recv()
    m_hop(4, False)

    coef = I64[...].reshape(64, RANK)
    coef = jnp.where(c == 0, coef, coef * coef)
    RT[...] = jnp.dot(coef, Ms[...], precision=lax.Precision.HIGHEST, preferred_element_type=F32)
    for rel in (1, 2, 3):
        r_copy(rel).start()
    Rr[c, yl] = RT[pl.ds(pl.multiple_of(k * 16, 16), 16)]

    z_step(4)
    for ry in (0, 1):
        for rel in range(4):
            if ry + rel > 0:
                remote(Ff.at[ry, rel], Ff.at[ry, rel], f_r.at[ry, rel], f_r.at[ry, rel], xl).wait_recv()
    for rel in range(4):
        gi_v[:, pl.ds(pl.multiple_of(mate(rel) * 128, 128), 128)] = Ff[0, rel] + Ff[1, rel]
    out_gi = pltpu.make_async_copy(gi_v, o_gi, loc.at[0])
    out_gi.start()

    for rel in (1, 2, 3):
        r_copy(rel).wait_recv()
    for h in (0, 1):
        cols = pl.ds(h * HALF, HALF)
        grad = Z[z, :, cols]
        first = 0.9 * Rr[0, h] + 0.1 * grad
        second = 0.95 * Rr[1, h] + 0.05 * grad * grad
        f_v[:, cols] = first
        s_v[:, cols] = second
        u_v[:, cols] = first / (jnp.sqrt(second) + 1e-8)

    outs = [out_gi]
    for i, (src, dst) in enumerate(((f_v, o_f), (s_v, o_s), (u_v, o_u))):
        outs.append(pltpu.make_async_copy(src, dst, loc.at[i + 1]))
        outs[-1].start()

    for j in (1, 2, 3, 4):
        for way in (0, 1):
            for h in (0, 1):
                if j < 4 or h == FIRST[way]:
                    w_copy(way, j, h).wait_send()
                    m_copy(way, j, h).wait_send()
    for h in (0, 1):
        for rel in (1, 2, 3):
            g_copy(rel, h).wait_send()
    for rel in (1, 2, 3):
        b_copy(rel).wait_send()
        sq_copy(rel).wait_send()
        nq_copy(rel).wait_send()
        ma_copy(rel, fm).wait_send()
        i_copy(rel).wait_send()
        r_copy(rel).wait_send()
    for j in range(4):
        for way in (0, 1):
            Tree(Z, ZR, COLS, z_s, z_r).copy(way, j).wait_send()
            Tree(Y, YR, RANK, y_s, y_r).copy(way, j).wait_send()
    run(drain, (5, 3, 0, 1))
    for cp in outs:
        cp.wait()


def hand_over(a, b, c, d, oa, ob, oc, od, va, vb, vc, vd, sem):
    triples = ((a, va, oa), (b, vb, ob), (c, vc, oc), (d, vd, od))
    for i, (src, mid, _) in enumerate(triples):
        pltpu.make_async_copy(src, mid, sem.at[0, i]).start()
    for i, (src, mid, dst) in enumerate(triples):
        pltpu.make_async_copy(src, mid, sem.at[0, i]).wait()
        pltpu.make_async_copy(mid, dst, sem.at[1, i]).start()
    for i, (_, mid, dst) in enumerate(triples):
        pltpu.make_async_copy(mid, dst, sem.at[1, i]).wait()


def per_device(grad_out, weight, saved, first_moment, second_moment, basis, new_basis):
    hbm = pl.BlockSpec(memory_space=pl.ANY)
    dma = pltpu.SemaphoreType.DMA
    rank = jax.ShapeDtypeStruct((ROWS, COLS), F32)
    results = pl.pallas_call(
        kernel,
        out_shape=(jax.ShapeDtypeStruct((TOK, RANK), F32), rank, rank, rank),
        in_specs=[hbm] * 7,
        out_specs=(hbm,) * 4,
        scratch_shapes=[
            pltpu.VMEM((TOK, RANK), BF16),
            pltpu.VMEM((DROWS, RANK), BF16),
            pltpu.VMEM((4, TOK, COLS), BF16),
            pltpu.VMEM((8, DROWS, COLS), BF16),
            pltpu.VMEM((8, 4, TOK, DROWS), F32),
            pltpu.VMEM((8, 4, DROWS, DROWS), F32),
            pltpu.VMEM((8, 4, DROWS, DROWS), F32),
            pltpu.VMEM((2, 4, TOK, DROWS), F32),
            pltpu.VMEM((8, 4, 16, TOK), BF16),
            pltpu.VMEM((4, 8, 16, TOK), BF16),
            pltpu.VMEM((8, 4, 16, DROWS), BF16),
            pltpu.VMEM((4, 8, 16, DROWS), BF16),
            pltpu.VMEM((4, DROWS, RANK), BF16),
            pltpu.VMEM((RANK, HALF), F32),
            pltpu.VMEM((8, 16, COLS), F32),
            pltpu.VMEM((2, 4, 16, COLS), F32),
            pltpu.VMEM((8, 16, RANK), F32),
            pltpu.VMEM((2, 4, 16, RANK), F32),
            pltpu.VMEM((4, 16, RANK), F32),
            pltpu.VMEM((64, HALF), F32),
            pltpu.VMEM((2, 2, 16, HALF), F32),
            pltpu.VMEM((TOK, RANK), F32),
            pltpu.VMEM((ROWS, COLS), F32),
            pltpu.VMEM((ROWS, COLS), F32),
            pltpu.VMEM((ROWS, COLS), F32),
            dma((6,)),
            dma((3, 2)),
            dma((3, 2)),
            dma((6, 3)),
            dma((6, 3)),
            dma((2, 4, 2)),
            dma((2, 4, 2)),
            dma((2, 4, 2)),
            dma((2, 4, 2)),
            dma((2, 4)),
            dma((2, 4)),
            dma((2, 4)),
            dma((2, 4)),
            dma((8,)),
            dma((8,)),
            dma((8, 4)),
            dma((8, 4)),
            dma((2, 4)),
            dma((2, 4)),
        ],
        compiler_params=pltpu.CompilerParams(
            collective_id=0, has_side_effects=True, vmem_limit_bytes=56 * 1024 * 1024
        ),
    )(grad_out, weight, saved, first_moment, second_moment, basis, new_basis)
    return pl.pallas_call(
        hand_over,
        out_shape=(jax.ShapeDtypeStruct((TOK, RANK), F32), rank, rank, rank),
        in_specs=[hbm] * 4,
        out_specs=(hbm,) * 4,
        scratch_shapes=[pltpu.VMEM((TOK, RANK), F32)] + [pltpu.VMEM((ROWS, COLS), F32)] * 3 + [dma((2, 4))],
    )(*results)


def solution(mesh):
    return jax.shard_map(
        per_device,
        mesh=mesh,
        in_specs=(
            P("seq", "tp"),
            P("seq", "tp"),
            P("seq", None),
            P("seq", "tp"),
            P("seq", "tp"),
            P("seq", None),
            P("seq", None),
        ),
        out_specs=(P("seq", "tp"), P("seq", "tp"), P("seq", "tp"), P("seq", "tp")),
        check_vma=False,
    )
```

```python
import jax
import jax.numpy as jnp
from jax import lax
from jax.experimental import pallas as pl
from jax.experimental.pallas import tpu as pltpu
from jax.sharding import PartitionSpec as P

MESH = pl.DeviceIdType.MESH
F32 = jnp.float32
BF16 = jnp.bfloat16
NZ = 8
TOK = 256
COLS = 1792
HALF = COLS // 2
RANK = 512
ROWS = 16
DROWS = 128


def rem(a, b):
    return lax.rem(a, jnp.int32(b))


def div(a, b):
    return lax.div(a, jnp.int32(b))


def kernel(
    go, w, sv_h, fm, sm, ba, nb_h,
    o_gi, o_f, o_s, o_u,
    sv, nb, Gs, Ws, Pp, Xa, Xb, Xc, Ff, St, Sq, Nt, Nq, Bs, Ms, Z, ZR, Y, YR, I64, RT, Rr, gi_v, f_v, s_v, u_v,
    loc, g_s, g_r, k_s, k_r, w_s, w_r, m_s, m_r, z_s, z_r, y_s, y_r, ix_s, ix_r, xa_s, xb_s, xa_r, xb_r, xc_s, xc_r, f_s, f_r,
):
    s = lax.axis_index("seq")
    t = lax.axis_index("tp")
    z, k = div(s, 4), rem(s, 4)
    yl, c = div(k, 2), rem(k, 2)
    x, yh = div(t, 2), rem(t, 2)

    def mate(rel):
        if isinstance(rel, int):
            a, b = rel // 2, rel % 2
        else:
            a, b = div(rel, 2), rem(rel, 2)
        return rem(yl + a, 2) * 2 + rem(c + b, 2)

    def group_dev(rel):
        return (z * 4 + mate(rel), t)

    zl = (rem(z + NZ - 1, NZ) * 4 + k, t)
    zr = (rem(z + 1, NZ) * 4 + k, t)
    xl = (s, rem(x + 3, 4) * 2 + yh)
    xr = (s, rem(x + 1, 4) * 2 + yh)

    own_rows = pl.ds(pl.multiple_of(z * 64 + k * 16, 16), 16)
    own_cols = pl.ds(pl.multiple_of(yl * HALF, 128), HALF)
    own_lanes = pl.ds(pl.multiple_of(x * 128, 128), 128)
    own_g = pltpu.make_async_copy(go, Gs.at[0], loc.at[0])
    own_w = pltpu.make_async_copy(w, Ws.at[pl.ds(0, DROWS)], loc.at[1])
    own_b = pltpu.make_async_copy(ba.at[:, own_lanes], Bs.at[0], loc.at[2])
    own_sv = pltpu.make_async_copy(sv_h, sv, loc.at[4])
    own_nb = pltpu.make_async_copy(nb_h, nb, loc.at[5])
    for cp in (own_g, own_w, own_sv, own_nb, own_b):
        cp.start()

    @pl.when(c == 0)
    def _():
        pltpu.make_async_copy(fm.at[:, own_cols], Ms.at[own_rows], loc.at[3]).start()

    @pl.when(c == 1)
    def _():
        pltpu.make_async_copy(sm.at[:, own_cols], Ms.at[own_rows], loc.at[3]).start()

    barrier = pltpu.get_barrier_semaphore()
    partners = [group_dev(1), group_dev(2), group_dev(3), zl, zr, xl, xr]
    partners.append((s, rem(x + 2, 4) * 2 + yh))
    partners += [(z * 4 + mate(r), x * 2 + (1 - yh)) for r in range(4)]
    for dev in partners:
        pl.semaphore_signal(barrier, inc=1, device_id=dev, device_id_type=MESH)
    pl.semaphore_wait(barrier, len(partners))

    def remote(src, dst, ss, rs, dev):
        return pltpu.make_async_remote_copy(
            src_ref=src, dst_ref=dst, send_sem=ss, recv_sem=rs, device_id=dev, device_id_type=MESH
        )

    def zslot(d):
        return 0 if d == 0 else (2 * d - 1 if d > 0 else -2 * d)

    def w_copy(way, j, h):
        sign = 1 if way == 0 else -1
        dst = 7 if j == 4 else zslot(sign * j)
        rows = pl.ds(h * 64, 64)
        src = w.at[rows] if j == 1 else Ws.at[pl.ds(zslot(sign * (j - 1)) * DROWS + h * 64, 64)]
        return remote(src, Ws.at[pl.ds(dst * DROWS + h * 64, 64)], w_s.at[way], w_r.at[way, j - 1, h],
                      zl if way == 0 else zr)

    def m_copy(way, j, h, arriving=False):
        dist = j if arriving else j - 1
        blk = rem(z + dist, NZ) if way == 0 else rem(z + NZ - dist, NZ)
        rows = pl.ds(pl.multiple_of(blk * 64 + h * 32, 32), 32)
        return remote(Ms.at[rows], Ms.at[rows], m_s.at[way], m_r.at[way, j - 1, h],
                      zl if way == 0 else zr)

    def g_copy(rel, h):
        rows = pl.ds(h * 128, 128)
        if rel == 3:
            return remote(Gs.at[2, rows], Gs.at[3, rows], g_s.at[0], g_r.at[2, h], group_dev(1))
        return remote(go.at[rows], Gs.at[rel, rows], g_s.at[0], g_r.at[rel - 1, h], group_dev(rel))

    def b_copy(rel):
        if rel == 3:
            return remote(Bs.at[2], Bs.at[3], k_s.at[0], k_r.at[0, 2], group_dev(1))
        return remote(ba.at[:, own_lanes], Bs.at[rel], k_s.at[0], k_r.at[0, rel - 1], group_dev(rel))

    def sq_copy(rel):
        return remote(St.at[:, mate(rel)], Sq.at[rel], k_s.at[1], k_r.at[1, rel - 1], group_dev(rel))

    def nq_copy(rel):
        return remote(Nt.at[:, mate(rel)], Nq.at[rel], k_s.at[2], k_r.at[2, rel - 1], group_dev(rel))

    def ma_copy(rel, moment):
        half = rem(yl + rel // 2, 2)
        cols = pl.ds(pl.multiple_of(half * HALF, 128), HALF)
        return remote(moment.at[:, cols], Ms.at[own_rows], k_s.at[3], k_r.at[3, rel - 1], group_dev(rel))

    def i_copy(rel):
        return remote(I64.at[k], I64.at[k], k_s.at[4], k_r.at[4, rel - 1], group_dev(rel))

    def ix_copy(step):
        return remote(Y.at[z], I64.at[k, x], ix_s.at[0], ix_r.at[step - 1], (s, rem(x + step, 4) * 2 + yh))

    def r_copy(rel):
        rows = pl.ds(pl.multiple_of(mate(rel) * 16, 16), 16)
        return remote(RT.at[rows], Rr.at[c, yl], k_s.at[5], k_r.at[5, rel - 1], group_dev(rel))

    def z_block(way, j):
        dist = 4 - j
        return rem(z + dist, NZ) if way == 1 else rem(z + NZ - dist, NZ)

    class Tree:
        def __init__(self, own, got, ss, rs):
            self.own, self.got, self.ss, self.rs = own, got, ss, rs

        def part(self, way, j):
            return pl.ds((1 - way) * 8, 8) if j == 0 else pl.ds(0, 16)

        def copy(self, way, j):
            part = self.part(way, j)
            return remote(self.own.at[z_block(way, j), part], self.got.at[way, j, part],
                          self.ss.at[way], self.rs.at[way, j], zl if way == 0 else zr)

        def step(self, j):
            for way in (0, 1):
                if j > 0:
                    self.copy(way, j - 1).wait_recv()
                    part = self.part(way, j - 1)
                    blk = z_block(way, j)
                    self.own[blk, part] = self.own[blk, part] + self.got[way, j - 1, part]
                if j < 4:
                    self.copy(way, j).start()

        def close(self):
            for way in (0, 1):
                sent = self.own.at[pl.ds(0, 7), pl.ds(0, 8)]
                remote(sent, sent, self.ss.at[way], self.ss.at[way], zl).wait_send()

    z_tree, i_tree = Tree(Z, ZR, z_s, z_r), Tree(Y, YR, y_s, y_r)
    z_step, i_step = z_tree.step, i_tree.step

    def cp_a(di, rel):
        return remote(Pp.at[di, rel, pl.ds(0, 128)], Xa.at[di, rel], xa_s.at[di], xa_r.at[di, rel], xl)

    def cp_b(di, rel):
        return remote(Pp.at[di, rel, pl.ds(128, 128)], Xb.at[di, rel], xb_s.at[di], xb_r.at[di, rel], xr)

    def cp_c(di, rel):
        return remote(Pp.at[di, rel], Xc.at[di - 5, rel], xc_s.at[di - 5, rel], xc_r.at[di - 5, rel],
                      (s, x * 2 + (1 - yh)))

    def cp_f(di, rel, zt, ry):
        return remote(Pp.at[di, rel], Ff.at[ry, rel], f_s.at[ry, rel], f_r.at[ry, rel], (z * 4 + mate(rel), zt))

    def where_to(di):
        mag = div(di + 1, 2)
        d = mag * (2 * rem(di, 2) - 1)
        zt = rem(z + d + NZ, NZ)
        role = rem(x - div(zt, 2) + 4, 4)
        return zt, role

    near = 5 + rem(z + 1, 2)
    far = 5 + rem(z, 2)

    def crossing(di, rel):
        zt, _ = where_to(di)
        ry = rem(rem(zt, 2) + yh, 2)
        early = jnp.logical_and(jnp.logical_or(di == 7, di == near), rel < 2)
        early = jnp.logical_or(early, jnp.logical_and(di == far, rel < 1))
        return jnp.logical_and(early, ry == 1), jnp.logical_and(early, ry == 0), early

    def in_ring(di, rel, role_is):
        away, _, _ = crossing(di, rel)
        return jnp.logical_and(jnp.logical_not(away), role_is)

    def take_a(di, rel):
        cp_a(di, rel).wait_recv()
        Pp[di, rel, pl.ds(0, 128)] = Pp[di, rel, pl.ds(0, 128)] + Xa[di, rel]

    def take_b(di, rel):
        cp_b(di, rel).wait_recv()
        Pp[di, rel, pl.ds(128, 128)] = Pp[di, rel, pl.ds(128, 128)] + Xb[di, rel]

    def w_rows(di, n):
        return Ws[pl.ds(pl.multiple_of(di * DROWS, DROWS), n)]

    def stage1(di, rel):
        Pp[di, rel] = lax.dot_general(Gs[rel], w_rows(di, DROWS), (((1,), (1,)), ((), ())), preferred_element_type=F32)
        launch(di, rel)

    def stage1_pair(dp, rel):
        di = 2 * dp - 1
        both = w_rows(di, 2 * DROWS)
        out = lax.dot_general(Gs[rel], both, (((1,), (1,)), ((), ())), preferred_element_type=F32)
        Pp[di, rel] = out[:, :DROWS]
        Pp[di + 1, rel] = out[:, DROWS:]
        launch(di, rel)
        launch(di + 1, rel)

    def launch(di, rel):
        _, role = where_to(di)
        away, _, early = crossing(di, rel)

        @pl.when(away)
        def _():
            cp_c(di, rel).start()

        @pl.when(jnp.logical_not(early))
        def _():
            enter(di, rel)

    def enter(di, rel):
        _, role = where_to(di)

        @pl.when(role == 3)
        def _():
            cp_a(di, rel).start()

        @pl.when(role == 1)
        def _():
            cp_b(di, rel).start()

    def merge(di, rel):
        _, home, _ = crossing(di, rel)

        @pl.when(home)
        def _():
            cp_c(di, rel).wait_recv()
            Pp[di, rel] = Pp[di, rel] + Xc[di - 5, rel]
            enter(di, rel)

    def stage2(di, rel):
        _, role = where_to(di)

        @pl.when(in_ring(di, rel, role == 2))
        def _():
            take_a(di, rel)
            cp_a(di, rel).start()
            take_b(di, rel)
            cp_b(di, rel).start()

    def stage3(di, rel):
        _, role = where_to(di)

        @pl.when(in_ring(di, rel, role == 1))
        def _():
            take_a(di, rel)
            cp_a(di, rel).start()

        @pl.when(in_ring(di, rel, role == 3))
        def _():
            take_b(di, rel)
            cp_b(di, rel).start()

    def stage4(di, rel):
        zt, role = where_to(di)

        @pl.when(in_ring(di, rel, role == 0))
        def _():
            cp_a(di, rel).wait_recv()
            cp_b(di, rel).wait_recv()
            ry = rem(rem(zt, 2) + yh, 2)
            local = ry + rel == 0
            upper = Pp[di, rel, pl.ds(0, 128)] + Xa[di, rel]
            lower = Pp[di, rel, pl.ds(128, 128)] + Xb[di, rel]

            @pl.when(local)
            def _():
                Ff[0, 0, pl.ds(0, 128)] = upper
                Ff[0, 0, pl.ds(128, 128)] = lower

            @pl.when(jnp.logical_not(local))
            def _():
                Pp[di, rel, pl.ds(0, 128)] = upper
                Pp[di, rel, pl.ds(128, 128)] = lower
                cp_f(di, rel, zt, ry).start()

    def drain(di, unused):
        zt, role = where_to(di)
        ry = rem(rem(zt, 2) + yh, 2)
        away0, _, _ = crossing(di, 0)
        away1, _, _ = crossing(di, 1)

        def ring_sends(cond, lo, n):
            @pl.when(jnp.logical_and(role > 0, cond))
            def _():
                upper = Pp.at[di, pl.ds(lo, n), pl.ds(0, 128)]
                lower = Pp.at[di, pl.ds(lo, n), pl.ds(128, 128)]
                remote(upper, upper, xa_s.at[di], xa_s.at[di], xl).wait_send()
                remote(lower, lower, xb_s.at[di], xb_s.at[di], xr).wait_send()

        ring_sends(away1, 2, 2)
        ring_sends(jnp.logical_and(away0, jnp.logical_not(away1)), 1, 3)
        ring_sends(jnp.logical_not(away0), 0, 4)

        @pl.when(away0)
        def _():
            cp_c(di, 0).wait_send()

        @pl.when(away1)
        def _():
            cp_c(di, 1).wait_send()

        @pl.when(role == 0)
        def _():
            for rel in (2, 3):
                cp_f(di, rel, zt, ry).wait_send()

            @pl.when(jnp.logical_not(away1))
            def _():
                cp_f(di, 1, zt, ry).wait_send()

            @pl.when(jnp.logical_and(jnp.logical_not(away0), ry > 0))
            def _():
                cp_f(di, 0, zt, ry).wait_send()

    def run(stage, group):
        d0, dn, r0, rn = group

        def step(i, carry):
            stage(d0 + div(i, rn), r0 + rem(i, rn))
            return carry

        lax.fori_loop(jnp.int32(0), jnp.int32(dn * rn), step, jnp.int32(0))

    A0, A1 = (0, 1, 0, 1), (0, 1, 1, 1)
    A, B, C, F = (0, 1, 0, 2), (1, 2, 0, 2), (3, 2, 0, 2), (7, 1, 0, 4)
    PB, PC, PD2, PD3, PE = (1, 1, 0, 2), (2, 1, 0, 2), (1, 1, 2, 2), (2, 1, 2, 2), (3, 1, 0, 4)
    D1, D2, D3 = (0, 1, 2, 2), (1, 2, 2, 2), (3, 2, 2, 2)
    E1, E2 = (near, 1, 2, 2), (far, 1, 1, 3)
    G0 = (far, 1, 0, 1)
    E0, F0, F1 = (near, 1, 0, 2), (7, 1, 0, 2), (7, 1, 2, 2)

    FIRST = {0: 0, 1: 1}

    def w_hop(j, second):
        for way in (0, 1):
            h = 1 - FIRST[way] if second else FIRST[way]
            if j == 4 and second:
                continue
            w_copy(way, j, h).wait_recv()
            if j < 3 or (j == 3 and not second):
                w_copy(way, j + 1, h).start()

    def m_hop(j, second):
        for way in (0, 1):
            h = 1 - FIRST[way] if second else FIRST[way]
            if j == 4 and second:
                continue
            m_copy(way, j, h, arriving=True).wait_recv()
            if j < 3 or (j == 3 and not second):
                m_copy(way, j + 1, h).start()

    for second in (False, True):
        for way in (0, 1):
            w_copy(way, 1, 1 - FIRST[way] if second else FIRST[way]).start()
    for rel in (1, 2, 3):
        other = rem(c + rel % 2, 2)

        @pl.when(other == 0)
        def _(rel=rel):
            ma_copy(rel, fm).start()

        @pl.when(other == 1)
        def _(rel=rel):
            ma_copy(rel, sm).start()

    g_copy(2, 0).start()
    for h in (0, 1):
        g_copy(1, h).start()
    own_nb.wait()
    Nt[...] = jnp.transpose(nb[...].astype(F32)).astype(BF16).reshape(8, 4, 16, DROWS)
    Nq[0] = Nt[:, k]
    for rel in (1, 2):
        b_copy(rel).start()
    for rel in (1, 2, 3):
        nq_copy(rel).start()
    g_copy(2, 1).start()
    own_sv.wait()
    St[...] = jnp.transpose(sv[...].astype(F32)).astype(BF16).reshape(8, 4, 16, TOK)
    Sq[0] = St[:, k]
    for rel in (1, 2, 3):
        sq_copy(rel).start()
    own_g.wait()
    own_w.wait()
    run(stage1, A0)
    for h in (0, 1):
        g_copy(1, h).wait_recv()
    run(stage1, A1)

    w_hop(1, False)
    run(stage2, A)
    w_hop(1, True)
    run(stage3, A)
    g_copy(2, 0).wait_recv()
    g_copy(3, 0).start()
    b_copy(2).wait_recv()
    b_copy(3).start()
    run(stage1_pair, PB)
    own_b.wait()
    b_copy(1).wait_recv()
    b_copy(3).wait_recv()
    for rel in (1, 2, 3):
        nq_copy(rel).wait_recv()
    inter = jnp.zeros((DROWS, 128), F32)
    for rel in range(4):
        inter += jnp.dot(Nq[rel].reshape(DROWS, DROWS), Bs[rel], preferred_element_type=F32)
    Y[...] = inter.reshape(8, 16, 128)
    i_step(0)
    w_hop(2, False)
    run(stage4, A)
    run(stage2, B)
    w_hop(2, True)
    run(stage1_pair, PC)
    run(stage3, B)
    g_copy(2, 1).wait_recv()
    g_copy(3, 1).start()
    g_copy(3, 0).wait_recv()
    g_copy(3, 1).wait_recv()
    run(stage1, D1)
    w_hop(3, False)
    run(stage1_pair, PD2)
    run(stage1_pair, PD3)
    i_step(1)
    run(stage2, C)

    for rel in (1, 2, 3):
        sq_copy(rel).wait_recv()

    def grad_tile(i, carry):
        cols = pl.ds(pl.multiple_of(i * 256, 256), 256)
        acc = jnp.zeros((DROWS, 256), F32)
        for rel in range(4):
            acc += jnp.dot(Sq[rel].reshape(DROWS, TOK), Gs[rel, :, cols], preferred_element_type=F32)
        Z[:, :, cols] = acc.reshape(8, 16, 256)
        return carry

    lax.fori_loop(jnp.int32(0), jnp.int32(COLS // 256), grad_tile, jnp.int32(0))
    z_step(0)
    for rel in (1, 2, 3):
        ma_copy(rel, fm).wait_recv()
    pltpu.make_async_copy(fm.at[:, own_cols], Ms.at[own_rows], loc.at[3]).wait()
    for second in (False, True):
        for way in (0, 1):
            m_copy(way, 1, 1 - FIRST[way] if second else FIRST[way]).start()
    run(stage2, D1)
    run(stage4, B)
    w_hop(3, True)
    run(stage1_pair, PE)
    run(stage3, C)
    run(stage2, D2)
    run(stage3, D1)
    run(stage2, D3)
    w_hop(4, False)
    run(stage1, F)
    z_step(1)
    i_step(2)
    run(stage2, E1)
    run(stage4, C)
    m_hop(1, False)
    run(stage2, E2)
    run(stage3, D2)
    run(stage4, D1)
    i_step(3)
    m_hop(1, True)
    run(stage2, F1)
    run(stage3, D3)
    run(stage3, E1)
    z_step(2)
    m_hop(2, False)
    i_step(4)
    I64[k, x] = Y[z]
    for step in (1, 2, 3):
        ix_copy(step).start()
    run(stage4, D2)
    run(merge, E0)
    run(stage3, F1)
    m_hop(2, True)
    run(merge, G0)
    run(stage3, E2)
    run(stage4, D3)
    run(merge, F0)
    run(stage2, E0)
    run(stage2, G0)
    run(stage4, E1)
    m_hop(3, False)
    z_step(3)
    for step in (1, 2, 3):
        ix_copy(step).wait_recv()
    for rel in (1, 2, 3):
        i_copy(rel).start()
    run(stage2, F0)
    run(stage4, E2)
    run(stage4, F1)
    run(stage3, E0)
    run(stage3, G0)
    m_hop(3, True)
    run(stage3, F0)
    run(drain, (0, 5, 0, 1))
    for rel in (1, 2, 3):
        i_copy(rel).wait_recv()
    m_hop(4, False)

    coef = jnp.concatenate([I64[:, i].reshape(64, 128) for i in range(4)], axis=1)
    coef = jnp.where(c == 0, coef, coef * coef)
    RT[...] = jnp.dot(coef, Ms[...], precision=lax.Precision.HIGHEST, preferred_element_type=F32)
    for rel in (1, 2, 3):
        r_copy(rel).start()
    run(stage4, E0)
    run(stage4, G0)
    run(stage4, F0)
    Rr[c, yl] = RT[pl.ds(pl.multiple_of(k * 16, 16), 16)]

    def piece(ry, rel):
        remote(Ff.at[ry, rel], Ff.at[ry, rel], f_r.at[ry, rel], f_r.at[ry, rel], xl).wait_recv()

    ahead = rem(t - z + NZ, NZ)
    merged = jnp.logical_or(ahead == 4, ahead == 5 - 2 * rem(z, 2))
    merged = (jnp.logical_or(merged, ahead == 3 + 2 * rem(z, 2)), merged)
    for rel in range(4):
        cols = pl.ds(pl.multiple_of(mate(rel) * 128, 128), 128)
        if rel > 0:
            piece(0, rel)
        if rel > 1:
            piece(1, rel)
            gi_v[:, cols] = Ff[0, rel] + Ff[1, rel]
        else:

            @pl.when(merged[rel])
            def _(rel=rel, cols=cols):
                gi_v[:, cols] = Ff[0, rel]

            @pl.when(jnp.logical_not(merged[rel]))
            def _(rel=rel, cols=cols):
                piece(1, rel)
                gi_v[:, cols] = Ff[0, rel] + Ff[1, rel]

    out_gi = pltpu.make_async_copy(gi_v, o_gi, loc.at[0])
    out_gi.start()

    z_step(4)
    for rel in (1, 2, 3):
        r_copy(rel).wait_recv()
    for h in (0, 1):
        cols = pl.ds(h * HALF, HALF)
        grad = Z[z, :, cols]
        first = 0.9 * Rr[0, h] + 0.1 * grad
        second = 0.95 * Rr[1, h] + 0.05 * grad * grad
        f_v[:, cols] = first
        s_v[:, cols] = second
        u_v[:, cols] = first / (jnp.sqrt(second) + 1e-8)

    outs = [out_gi]
    for i, (src, dst) in enumerate(((f_v, o_f), (s_v, o_s), (u_v, o_u))):
        outs.append(pltpu.make_async_copy(src, dst, loc.at[i + 1]))
        outs[-1].start()

    def sent(ref, sem):
        remote(ref, ref, sem, sem, zl).wait_send()

    for way in (0, 1):
        sent(Ws.at[pl.ds(0, 448)], w_s.at[way])
        sent(Ms.at[pl.ds(0, 224)], m_s.at[way])
    sent(Gs.at[pl.ds(0, 3)], g_s.at[0])
    z_tree.close()
    i_tree.close()
    three = pl.ds(1, 3)
    rows48 = pl.ds(0, 48)
    for kind, ref in enumerate((Bs.at[three], Sq.at[three], Nq.at[three], Ms.at[rows48], I64.at[three], RT.at[rows48])):
        sent(ref, k_s.at[kind])
    sent(Y.at[pl.ds(0, 3)], ix_s.at[0])
    run(drain, (5, 3, 0, 1))
    for cp in outs:
        cp.wait()


def hand_over(a, b, c, d, oa, ob, oc, od, va, vb, vc, vd, sem):
    triples = ((a, va, oa), (b, vb, ob), (c, vc, oc), (d, vd, od))
    for i, (src, mid, _) in enumerate(triples):
        pltpu.make_async_copy(src, mid, sem.at[0, i]).start()
    for i, (src, mid, dst) in enumerate(triples):
        pltpu.make_async_copy(src, mid, sem.at[0, i]).wait()
        pltpu.make_async_copy(mid, dst, sem.at[1, i]).start()
    for i, (_, mid, dst) in enumerate(triples):
        pltpu.make_async_copy(mid, dst, sem.at[1, i]).wait()


def per_device(grad_out, weight, saved, first_moment, second_moment, basis, new_basis):
    hbm = pl.BlockSpec(memory_space=pl.ANY)
    dma = pltpu.SemaphoreType.DMA
    rank = jax.ShapeDtypeStruct((ROWS, COLS), F32)
    results = pl.pallas_call(
        kernel,
        out_shape=(jax.ShapeDtypeStruct((TOK, RANK), F32), rank, rank, rank),
        in_specs=[hbm] * 7,
        out_specs=(hbm,) * 4,
        scratch_shapes=[
            pltpu.VMEM((TOK, RANK), BF16),
            pltpu.VMEM((DROWS, RANK), BF16),
            pltpu.VMEM((4, TOK, COLS), BF16),
            pltpu.VMEM((8 * DROWS, COLS), BF16),
            pltpu.VMEM((8, 4, TOK, DROWS), F32),
            pltpu.VMEM((8, 4, DROWS, DROWS), F32),
            pltpu.VMEM((8, 4, DROWS, DROWS), F32),
            pltpu.VMEM((3, 2, TOK, DROWS), F32),
            pltpu.VMEM((2, 4, TOK, DROWS), F32),
            pltpu.VMEM((8, 4, 16, TOK), BF16),
            pltpu.VMEM((4, 8, 16, TOK), BF16),
            pltpu.VMEM((8, 4, 16, DROWS), BF16),
            pltpu.VMEM((4, 8, 16, DROWS), BF16),
            pltpu.VMEM((4, DROWS, 128), BF16),
            pltpu.VMEM((RANK, HALF), F32),
            pltpu.VMEM((8, 16, COLS), F32),
            pltpu.VMEM((2, 4, 16, COLS), F32),
            pltpu.VMEM((8, 16, 128), F32),
            pltpu.VMEM((2, 4, 16, 128), F32),
            pltpu.VMEM((4, 4, 16, 128), F32),
            pltpu.VMEM((64, HALF), F32),
            pltpu.VMEM((2, 2, 16, HALF), F32),
            pltpu.VMEM((TOK, RANK), F32),
            pltpu.VMEM((ROWS, COLS), F32),
            pltpu.VMEM((ROWS, COLS), F32),
            pltpu.VMEM((ROWS, COLS), F32),
            dma((6,)),
            dma((1,)),
            dma((3, 2)),
            dma((6,)),
            dma((6, 3)),
            dma((2,)),
            dma((2, 4, 2)),
            dma((2,)),
            dma((2, 4, 2)),
            dma((2,)),
            dma((2, 4)),
            dma((2,)),
            dma((2, 4)),
            dma((1,)),
            dma((3,)),
            dma((8,)),
            dma((8,)),
            dma((8, 4)),
            dma((8, 4)),
            dma((3, 2)),
            dma((3, 2)),
            dma((2, 4)),
            dma((2, 4)),
        ],
        compiler_params=pltpu.CompilerParams(
            collective_id=0, has_side_effects=True, vmem_limit_bytes=56 * 1024 * 1024
        ),
    )(grad_out, weight, saved, first_moment, second_moment, basis, new_basis)
    return pl.pallas_call(
        hand_over,
        out_shape=(jax.ShapeDtypeStruct((TOK, RANK), F32), rank, rank, rank),
        in_specs=[hbm] * 4,
        out_specs=(hbm,) * 4,
        scratch_shapes=[pltpu.VMEM((TOK, RANK), F32)] + [pltpu.VMEM((ROWS, COLS), F32)] * 3 + [dma((2, 4))],
    )(*results)


def solution(mesh):
    return jax.shard_map(
        per_device,
        mesh=mesh,
        in_specs=(
            P("seq", "tp"),
            P("seq", "tp"),
            P("seq", None),
            P("seq", "tp"),
            P("seq", "tp"),
            P("seq", None),
            P("seq", None),
        ),
        out_specs=(P("seq", "tp"), P("seq", "tp"), P("seq", "tp"), P("seq", "tp")),
        check_vma=False,
    )
```

```python
import jax
import jax.numpy as jnp
from jax import lax
from jax.experimental import pallas as pl
from jax.experimental.pallas import tpu as pltpu
from jax.sharding import PartitionSpec as P

MESH = pl.DeviceIdType.MESH
F32 = jnp.float32
BF16 = jnp.bfloat16
NZ = 8
TOK = 256
COLS = 1792
HALF = COLS // 2
RANK = 512
ROWS = 16
DROWS = 128


def rem(a, b):
    return lax.rem(a, jnp.int32(b))


def div(a, b):
    return lax.div(a, jnp.int32(b))


def kernel(
    go, w, sv_h, fm, sm, ba, nb_h,
    o_gi, o_f, o_s, o_u,
    sv, nb, Gs, Ws, Pp, Xa, Xb, Xc, Ff, St, Sq, Nt, Nq, Bs, Ms, Z, ZR, Y, YR, I64, RT, Rr, gi_v, f_v, s_v, u_v,
    loc, g_s, g_r, k_s, k_r, w_s, w_r, m_s, m_r, z_s, z_r, y_s, y_r, ix_s, ix_r, xa_s, xb_s, xa_r, xb_r, xc_s, xc_r, f_s, f_r,
):
    s = lax.axis_index("seq")
    t = lax.axis_index("tp")
    z, k = div(s, 4), rem(s, 4)
    yl, c = div(k, 2), rem(k, 2)
    x, yh = div(t, 2), rem(t, 2)

    def mate(rel):
        if isinstance(rel, int):
            a, b = rel // 2, rel % 2
        else:
            a, b = div(rel, 2), rem(rel, 2)
        return rem(yl + a, 2) * 2 + rem(c + b, 2)

    def group_dev(rel):
        return (z * 4 + mate(rel), t)

    zl = (rem(z + NZ - 1, NZ) * 4 + k, t)
    zr = (rem(z + 1, NZ) * 4 + k, t)
    xl = (s, rem(x + 3, 4) * 2 + yh)
    xr = (s, rem(x + 1, 4) * 2 + yh)

    own_rows = pl.ds(pl.multiple_of(z * 64 + k * 16, 16), 16)
    own_cols = pl.ds(pl.multiple_of(yl * HALF, 128), HALF)
    own_lanes = pl.ds(pl.multiple_of(x * 128, 128), 128)
    own_g = pltpu.make_async_copy(go, Gs.at[0], loc.at[0])
    own_w = pltpu.make_async_copy(w, Ws.at[pl.ds(0, DROWS)], loc.at[1])
    own_b = pltpu.make_async_copy(ba.at[:, own_lanes], Bs.at[0], loc.at[2])
    own_sv = pltpu.make_async_copy(sv_h, sv, loc.at[4])
    own_nb = pltpu.make_async_copy(nb_h, nb, loc.at[5])
    for cp in (own_g, own_w, own_sv, own_nb, own_b):
        cp.start()

    @pl.when(c == 0)
    def _():
        pltpu.make_async_copy(fm.at[:, own_cols], Ms.at[own_rows], loc.at[3]).start()

    @pl.when(c == 1)
    def _():
        pltpu.make_async_copy(sm.at[:, own_cols], Ms.at[own_rows], loc.at[3]).start()

    barrier = pltpu.get_barrier_semaphore()
    partners = [group_dev(1), group_dev(2), group_dev(3), zl, zr, xl, xr]
    partners.append((s, rem(x + 2, 4) * 2 + yh))
    partners += [(z * 4 + mate(r), x * 2 + (1 - yh)) for r in range(4)]
    for dev in partners:
        pl.semaphore_signal(barrier, inc=1, device_id=dev, device_id_type=MESH)
    pl.semaphore_wait(barrier, len(partners))

    def remote(src, dst, ss, rs, dev):
        return pltpu.make_async_remote_copy(
            src_ref=src, dst_ref=dst, send_sem=ss, recv_sem=rs, device_id=dev, device_id_type=MESH
        )

    def zslot(d):
        return 0 if d == 0 else (2 * d - 1 if d > 0 else -2 * d)

    def w_copy(way, j, h):
        sign = 1 if way == 0 else -1
        dst = 7 if j == 4 else zslot(sign * j)
        rows = pl.ds(h * 64, 64)
        src = w.at[rows] if j == 1 else Ws.at[pl.ds(zslot(sign * (j - 1)) * DROWS + h * 64, 64)]
        return remote(src, Ws.at[pl.ds(dst * DROWS + h * 64, 64)], w_s.at[way], w_r.at[way, j - 1, h],
                      zl if way == 0 else zr)

    def m_copy(way, j, h, arriving=False):
        dist = j if arriving else j - 1
        blk = rem(z + dist, NZ) if way == 0 else rem(z + NZ - dist, NZ)
        rows = pl.ds(pl.multiple_of(blk * 64 + h * 32, 32), 32)
        return remote(Ms.at[rows], Ms.at[rows], m_s.at[way], m_r.at[way, j - 1, h],
                      zl if way == 0 else zr)

    def g_copy(rel, h):
        rows = pl.ds(h * 128, 128)
        if rel == 3:
            return remote(Gs.at[2, rows], Gs.at[3, rows], g_s.at[0], g_r.at[2, h], group_dev(1))
        return remote(go.at[rows], Gs.at[rel, rows], g_s.at[0], g_r.at[rel - 1, h], group_dev(rel))

    def b_copy(rel):
        if rel == 3:
            return remote(Bs.at[2], Bs.at[3], k_s.at[0], k_r.at[0, 2], group_dev(1))
        return remote(ba.at[:, own_lanes], Bs.at[rel], k_s.at[0], k_r.at[0, rel - 1], group_dev(rel))

    def sq_copy(rel):
        return remote(St.at[:, mate(rel)], Sq.at[rel], k_s.at[1], k_r.at[1, rel - 1], group_dev(rel))

    def nq_copy(rel):
        return remote(Nt.at[:, mate(rel)], Nq.at[rel], k_s.at[2], k_r.at[2, rel - 1], group_dev(rel))

    def ma_copy(rel, moment):
        half = rem(yl + rel // 2, 2)
        cols = pl.ds(pl.multiple_of(half * HALF, 128), HALF)
        return remote(moment.at[:, cols], Ms.at[own_rows], k_s.at[3], k_r.at[3, rel - 1], group_dev(rel))

    def i_copy(rel):
        return remote(I64.at[k], I64.at[k], k_s.at[4], k_r.at[4, rel - 1], group_dev(rel))

    def ix_copy(step):
        return remote(Y.at[z], I64.at[k, x], ix_s.at[0], ix_r.at[step - 1], (s, rem(x + step, 4) * 2 + yh))

    PARTS = (pl.ds(0, 512), pl.ds(512, HALF - 512))

    def r_copy(rel, part):
        cols = PARTS[part]
        rows = pl.ds(pl.multiple_of(mate(rel) * 16, 16), 16)
        return remote(RT.at[rows, cols], Rr.at[c, yl, :, cols], k_s.at[5], k_r.at[5 + part, rel - 1], group_dev(rel))

    def z_block(way, j):
        dist = 4 - j
        return rem(z + dist, NZ) if way == 1 else rem(z + NZ - dist, NZ)

    class Tree:
        def __init__(self, own, got, ss, rs):
            self.own, self.got, self.ss, self.rs = own, got, ss, rs

        def part(self, way, j):
            return pl.ds((1 - way) * 8, 8) if j == 0 else pl.ds(0, 16)

        def copy(self, way, j):
            part = self.part(way, j)
            return remote(self.own.at[z_block(way, j), part], self.got.at[way, j, part],
                          self.ss.at[way], self.rs.at[way, j], zl if way == 0 else zr)

        def step(self, j):
            for way in (0, 1):
                if j > 0:
                    self.copy(way, j - 1).wait_recv()
                    part = self.part(way, j - 1)
                    blk = z_block(way, j)
                    self.own[blk, part] = self.own[blk, part] + self.got[way, j - 1, part]
                if j < 4:
                    self.copy(way, j).start()

        def close(self):
            for way in (0, 1):
                sent = self.own.at[pl.ds(0, 7), pl.ds(0, 8)]
                remote(sent, sent, self.ss.at[way], self.ss.at[way], zl).wait_send()

    z_tree, i_tree = Tree(Z, ZR, z_s, z_r), Tree(Y, YR, y_s, y_r)
    z_step, i_step = z_tree.step, i_tree.step

    def cp_a(di, rel):
        return remote(Pp.at[di, rel, pl.ds(0, 128)], Xa.at[di, rel], xa_s.at[di], xa_r.at[di, rel], xl)

    def cp_b(di, rel):
        return remote(Pp.at[di, rel, pl.ds(128, 128)], Xb.at[di, rel], xb_s.at[di], xb_r.at[di, rel], xr)

    def cp_c(di, rel):
        return remote(Pp.at[di, rel], Xc.at[di - 5, rel], xc_s.at[di - 5, rel], xc_r.at[di - 5, rel],
                      (s, x * 2 + (1 - yh)))

    def cp_f(di, rel, zt, ry):
        return remote(Pp.at[di, rel], Ff.at[ry, rel], f_s.at[ry, rel], f_r.at[ry, rel], (z * 4 + mate(rel), zt))

    def where_to(di):
        mag = div(di + 1, 2)
        d = mag * (2 * rem(di, 2) - 1)
        zt = rem(z + d + NZ, NZ)
        role = rem(x - div(zt, 2) + 4, 4)
        return zt, role

    near = 5 + rem(z + 1, 2)
    far = 5 + rem(z, 2)

    def crossing(di, rel):
        zt, _ = where_to(di)
        ry = rem(rem(zt, 2) + yh, 2)
        early = jnp.logical_and(jnp.logical_or(di == 7, di == near), rel < 2)
        early = jnp.logical_or(early, jnp.logical_and(di == far, rel < 1))
        return jnp.logical_and(early, ry == 1), jnp.logical_and(early, ry == 0), early

    def in_ring(di, rel, role_is):
        away, _, _ = crossing(di, rel)
        return jnp.logical_and(jnp.logical_not(away), role_is)

    def take_a(di, rel):
        cp_a(di, rel).wait_recv()
        Pp[di, rel, pl.ds(0, 128)] = Pp[di, rel, pl.ds(0, 128)] + Xa[di, rel]

    def take_b(di, rel):
        cp_b(di, rel).wait_recv()
        Pp[di, rel, pl.ds(128, 128)] = Pp[di, rel, pl.ds(128, 128)] + Xb[di, rel]

    def w_rows(di, n):
        return Ws[pl.ds(pl.multiple_of(di * DROWS, DROWS), n)]

    def stage1(di, rel):
        Pp[di, rel] = lax.dot_general(Gs[rel], w_rows(di, DROWS), (((1,), (1,)), ((), ())), preferred_element_type=F32)
        launch(di, rel)

    def stage1_pair(dp, rel):
        di = 2 * dp - 1
        both = w_rows(di, 2 * DROWS)
        out = lax.dot_general(Gs[rel], both, (((1,), (1,)), ((), ())), preferred_element_type=F32)
        Pp[di, rel] = out[:, :DROWS]
        Pp[di + 1, rel] = out[:, DROWS:]
        launch(di, rel)
        launch(di + 1, rel)

    def launch(di, rel):
        _, role = where_to(di)
        away, _, early = crossing(di, rel)

        @pl.when(away)
        def _():
            cp_c(di, rel).start()

        @pl.when(jnp.logical_not(early))
        def _():
            enter(di, rel)

    def enter(di, rel):
        _, role = where_to(di)

        @pl.when(role == 3)
        def _():
            cp_a(di, rel).start()

        @pl.when(role == 1)
        def _():
            cp_b(di, rel).start()

    def merge(di, rel):
        _, home, _ = crossing(di, rel)

        @pl.when(home)
        def _():
            cp_c(di, rel).wait_recv()
            Pp[di, rel] = Pp[di, rel] + Xc[di - 5, rel]
            enter(di, rel)

    def stage2(di, rel):
        _, role = where_to(di)

        @pl.when(in_ring(di, rel, role == 2))
        def _():
            take_a(di, rel)
            cp_a(di, rel).start()
            take_b(di, rel)
            cp_b(di, rel).start()

    def stage3(di, rel):
        _, role = where_to(di)

        @pl.when(in_ring(di, rel, role == 1))
        def _():
            take_a(di, rel)
            cp_a(di, rel).start()

        @pl.when(in_ring(di, rel, role == 3))
        def _():
            take_b(di, rel)
            cp_b(di, rel).start()

    def stage4(di, rel):
        zt, role = where_to(di)

        @pl.when(in_ring(di, rel, role == 0))
        def _():
            cp_a(di, rel).wait_recv()
            cp_b(di, rel).wait_recv()
            ry = rem(rem(zt, 2) + yh, 2)
            local = ry + rel == 0
            upper = Pp[di, rel, pl.ds(0, 128)] + Xa[di, rel]
            lower = Pp[di, rel, pl.ds(128, 128)] + Xb[di, rel]

            @pl.when(local)
            def _():
                Ff[0, 0, pl.ds(0, 128)] = upper
                Ff[0, 0, pl.ds(128, 128)] = lower

            @pl.when(jnp.logical_not(local))
            def _():
                Pp[di, rel, pl.ds(0, 128)] = upper
                Pp[di, rel, pl.ds(128, 128)] = lower
                cp_f(di, rel, zt, ry).start()

    def drain(di, unused):
        zt, role = where_to(di)
        ry = rem(rem(zt, 2) + yh, 2)
        away0, _, _ = crossing(di, 0)
        away1, _, _ = crossing(di, 1)

        def ring_sends(cond, lo, n):
            @pl.when(jnp.logical_and(role > 0, cond))
            def _():
                upper = Pp.at[di, pl.ds(lo, n), pl.ds(0, 128)]
                lower = Pp.at[di, pl.ds(lo, n), pl.ds(128, 128)]
                remote(upper, upper, xa_s.at[di], xa_s.at[di], xl).wait_send()
                remote(lower, lower, xb_s.at[di], xb_s.at[di], xr).wait_send()

        ring_sends(away1, 2, 2)
        ring_sends(jnp.logical_and(away0, jnp.logical_not(away1)), 1, 3)
        ring_sends(jnp.logical_not(away0), 0, 4)

        @pl.when(away0)
        def _():
            cp_c(di, 0).wait_send()

        @pl.when(away1)
        def _():
            cp_c(di, 1).wait_send()

        @pl.when(role == 0)
        def _():
            for rel in (2, 3):
                cp_f(di, rel, zt, ry).wait_send()

            @pl.when(jnp.logical_not(away1))
            def _():
                cp_f(di, 1, zt, ry).wait_send()

            @pl.when(jnp.logical_and(jnp.logical_not(away0), ry > 0))
            def _():
                cp_f(di, 0, zt, ry).wait_send()

    def run(stage, group):
        d0, dn, r0, rn = group

        def step(i, carry):
            stage(d0 + div(i, rn), r0 + rem(i, rn))
            return carry

        lax.fori_loop(jnp.int32(0), jnp.int32(dn * rn), step, jnp.int32(0))

    A0, A1 = (0, 1, 0, 1), (0, 1, 1, 1)
    A, B, C, F = (0, 1, 0, 2), (1, 2, 0, 2), (3, 2, 0, 2), (7, 1, 0, 4)
    PB, PC, PD2, PD3, PE = (1, 1, 0, 2), (2, 1, 0, 2), (1, 1, 2, 2), (2, 1, 2, 2), (3, 1, 0, 4)
    D1, D2, D3 = (0, 1, 2, 2), (1, 2, 2, 2), (3, 2, 2, 2)
    E1, E2 = (near, 1, 2, 2), (far, 1, 1, 3)
    G0 = (far, 1, 0, 1)
    E0, F0, F1 = (near, 1, 0, 2), (7, 1, 0, 2), (7, 1, 2, 2)

    FIRST = {0: 0, 1: 1}

    def w_hop(j, second):
        for way in (0, 1):
            h = 1 - FIRST[way] if second else FIRST[way]
            if j == 4 and second:
                continue
            w_copy(way, j, h).wait_recv()
            if j < 3 or (j == 3 and not second):
                w_copy(way, j + 1, h).start()

    def m_hop(j, second):
        for way in (0, 1):
            h = 1 - FIRST[way] if second else FIRST[way]
            if j == 4 and second:
                continue
            m_copy(way, j, h, arriving=True).wait_recv()
            if j < 3 or (j == 3 and not second):
                m_copy(way, j + 1, h).start()

    for second in (False, True):
        for way in (0, 1):
            w_copy(way, 1, 1 - FIRST[way] if second else FIRST[way]).start()
    for rel in (1, 2, 3):
        other = rem(c + rel % 2, 2)

        @pl.when(other == 0)
        def _(rel=rel):
            ma_copy(rel, fm).start()

        @pl.when(other == 1)
        def _(rel=rel):
            ma_copy(rel, sm).start()

    g_copy(2, 0).start()
    for h in (0, 1):
        g_copy(1, h).start()
    own_nb.wait()
    Nt[...] = jnp.transpose(nb[...].astype(F32)).astype(BF16).reshape(8, 4, 16, DROWS)
    Nq[0] = Nt[:, k]
    for rel in (1, 2):
        b_copy(rel).start()
    for rel in (1, 2, 3):
        nq_copy(rel).start()
    g_copy(2, 1).start()
    own_sv.wait()
    St[...] = jnp.transpose(sv[...].astype(F32)).astype(BF16).reshape(8, 4, 16, TOK)
    Sq[0] = St[:, k]
    for rel in (1, 2, 3):
        sq_copy(rel).start()
    own_g.wait()
    own_w.wait()
    run(stage1, A0)
    for h in (0, 1):
        g_copy(1, h).wait_recv()
    run(stage1, A1)

    w_hop(1, False)
    run(stage2, A)
    w_hop(1, True)
    run(stage3, A)
    g_copy(2, 0).wait_recv()
    g_copy(3, 0).start()
    b_copy(2).wait_recv()
    b_copy(3).start()
    run(stage1_pair, PB)
    own_b.wait()
    b_copy(1).wait_recv()
    b_copy(3).wait_recv()
    for rel in (1, 2, 3):
        nq_copy(rel).wait_recv()
    inter = jnp.zeros((DROWS, 128), F32)
    for rel in range(4):
        inter += jnp.dot(Nq[rel].reshape(DROWS, DROWS), Bs[rel], preferred_element_type=F32)
    Y[...] = inter.reshape(8, 16, 128)
    i_step(0)
    w_hop(2, False)
    run(stage4, A)
    run(stage2, B)
    w_hop(2, True)
    run(stage1_pair, PC)
    run(stage3, B)
    g_copy(2, 1).wait_recv()
    g_copy(3, 1).start()
    g_copy(3, 0).wait_recv()
    g_copy(3, 1).wait_recv()
    run(stage1, D1)
    w_hop(3, False)
    run(stage1_pair, PD2)
    run(stage1_pair, PD3)
    i_step(1)
    run(stage2, C)

    for rel in (1, 2, 3):
        sq_copy(rel).wait_recv()

    def grad_tile(i, carry):
        cols = pl.ds(pl.multiple_of(i * 256, 256), 256)
        acc = jnp.zeros((DROWS, 256), F32)
        for rel in range(4):
            acc += jnp.dot(Sq[rel].reshape(DROWS, TOK), Gs[rel, :, cols], preferred_element_type=F32)
        Z[:, :, cols] = acc.reshape(8, 16, 256)
        return carry

    lax.fori_loop(jnp.int32(0), jnp.int32(COLS // 256), grad_tile, jnp.int32(0))
    z_step(0)
    for rel in (1, 2, 3):
        ma_copy(rel, fm).wait_recv()
    pltpu.make_async_copy(fm.at[:, own_cols], Ms.at[own_rows], loc.at[3]).wait()
    for second in (False, True):
        for way in (0, 1):
            m_copy(way, 1, 1 - FIRST[way] if second else FIRST[way]).start()
    run(stage2, D1)
    run(stage4, B)
    w_hop(3, True)
    run(stage1_pair, PE)
    run(stage3, C)
    run(stage2, D2)
    run(stage3, D1)
    run(stage2, D3)
    w_hop(4, False)
    run(stage1, F)
    z_step(1)
    i_step(2)
    run(stage2, E1)
    run(stage4, C)
    m_hop(1, False)
    run(stage2, E2)
    run(stage3, D2)
    run(stage4, D1)
    i_step(3)
    m_hop(1, True)
    run(stage2, F1)
    run(stage3, D3)
    run(stage3, E1)
    z_step(2)
    m_hop(2, False)
    i_step(4)
    I64[k, x] = Y[z]
    for step in (1, 2, 3):
        ix_copy(step).start()
    run(stage4, D2)
    run(merge, E0)
    run(stage3, F1)
    m_hop(2, True)
    run(merge, G0)
    run(stage3, E2)
    run(stage4, D3)
    run(merge, F0)
    run(stage2, E0)
    run(stage2, G0)
    run(stage4, E1)
    m_hop(3, False)
    z_step(3)
    for step in (1, 2, 3):
        ix_copy(step).wait_recv()
    for rel in (1, 2, 3):
        i_copy(rel).start()
    run(stage2, F0)
    run(stage4, E2)
    run(stage4, F1)
    run(stage3, E0)
    run(stage3, G0)
    m_hop(3, True)
    run(stage3, F0)
    run(drain, (0, 5, 0, 1))
    for rel in (1, 2, 3):
        i_copy(rel).wait_recv()
    m_hop(4, False)

    coef = jnp.concatenate([I64[:, i].reshape(64, 128) for i in range(4)], axis=1)
    coef = jnp.where(c == 0, coef, coef * coef)
    for part, cols in enumerate(PARTS):
        RT[:, cols] = jnp.dot(coef, Ms[:, cols], precision=lax.Precision.HIGHEST, preferred_element_type=F32)
        for rel in (2, 3, 1):
            r_copy(rel, part).start()
    run(stage4, E0)
    run(stage4, G0)
    run(stage4, F0)
    Rr[c, yl] = RT[pl.ds(pl.multiple_of(k * 16, 16), 16)]

    def piece(ry, rel):
        remote(Ff.at[ry, rel], Ff.at[ry, rel], f_r.at[ry, rel], f_r.at[ry, rel], xl).wait_recv()

    ahead = rem(t - z + NZ, NZ)
    merged = jnp.logical_or(ahead == 4, ahead == 5 - 2 * rem(z, 2))
    merged = (jnp.logical_or(merged, ahead == 3 + 2 * rem(z, 2)), merged)
    for rel in range(4):
        cols = pl.ds(pl.multiple_of(mate(rel) * 128, 128), 128)
        if rel > 0:
            piece(0, rel)
        if rel > 1:
            piece(1, rel)
            gi_v[:, cols] = Ff[0, rel] + Ff[1, rel]
        else:

            @pl.when(merged[rel])
            def _(rel=rel, cols=cols):
                gi_v[:, cols] = Ff[0, rel]

            @pl.when(jnp.logical_not(merged[rel]))
            def _(rel=rel, cols=cols):
                piece(1, rel)
                gi_v[:, cols] = Ff[0, rel] + Ff[1, rel]

    out_gi = pltpu.make_async_copy(gi_v, o_gi, loc.at[0])
    out_gi.start()

    z_step(4)
    for rel in (1, 2, 3):
        r_copy(rel, 0).wait_recv()
        r_copy(rel, 1).wait_recv()
    for h in (0, 1):
        cols = pl.ds(h * HALF, HALF)
        grad = Z[z, :, cols]
        first = 0.9 * Rr[0, h] + 0.1 * grad
        second = 0.95 * Rr[1, h] + 0.05 * grad * grad
        f_v[:, cols] = first
        s_v[:, cols] = second
        u_v[:, cols] = first / (jnp.sqrt(second) + 1e-8)

    outs = [out_gi]
    for i, (src, dst) in enumerate(((f_v, o_f), (s_v, o_s), (u_v, o_u))):
        outs.append(pltpu.make_async_copy(src, dst, loc.at[i + 1]))
        outs[-1].start()

    def sent(ref, sem):
        remote(ref, ref, sem, sem, zl).wait_send()

    for way in (0, 1):
        sent(Ws.at[pl.ds(0, 448)], w_s.at[way])
        sent(Ms.at[pl.ds(0, 224)], m_s.at[way])
    sent(Gs.at[pl.ds(0, 3)], g_s.at[0])
    z_tree.close()
    i_tree.close()
    three = pl.ds(1, 3)
    rows48 = pl.ds(0, 48)
    for kind, ref in enumerate((Bs.at[three], Sq.at[three], Nq.at[three], Ms.at[rows48], I64.at[three], RT.at[rows48])):
        sent(ref, k_s.at[kind])
    sent(Y.at[pl.ds(0, 3)], ix_s.at[0])
    run(drain, (5, 3, 0, 1))
    for cp in outs:
        cp.wait()


def hand_over(a, b, c, d, oa, ob, oc, od, va, vb, vc, vd, sem):
    triples = [tuple(ref.at[pl.ds(i * 64, 64)] for ref in (a, va, oa)) for i in range(4)]
    triples += [(b, vb, ob), (c, vc, oc), (d, vd, od)]
    for i, (src, mid, _) in enumerate(triples):
        pltpu.make_async_copy(src, mid, sem.at[0, i]).start()
    for i, (src, mid, dst) in enumerate(triples):
        pltpu.make_async_copy(src, mid, sem.at[0, i]).wait()
        pltpu.make_async_copy(mid, dst, sem.at[1, i]).start()
    for i, (_, mid, dst) in enumerate(triples):
        pltpu.make_async_copy(mid, dst, sem.at[1, i]).wait()


def per_device(grad_out, weight, saved, first_moment, second_moment, basis, new_basis):
    hbm = pl.BlockSpec(memory_space=pl.ANY)
    dma = pltpu.SemaphoreType.DMA
    rank = jax.ShapeDtypeStruct((ROWS, COLS), F32)
    results = pl.pallas_call(
        kernel,
        out_shape=(jax.ShapeDtypeStruct((TOK, RANK), F32), rank, rank, rank),
        in_specs=[hbm] * 7,
        out_specs=(hbm,) * 4,
        scratch_shapes=[
            pltpu.VMEM((TOK, RANK), BF16),
            pltpu.VMEM((DROWS, RANK), BF16),
            pltpu.VMEM((4, TOK, COLS), BF16),
            pltpu.VMEM((8 * DROWS, COLS), BF16),
            pltpu.VMEM((8, 4, TOK, DROWS), F32),
            pltpu.VMEM((8, 4, DROWS, DROWS), F32),
            pltpu.VMEM((8, 4, DROWS, DROWS), F32),
            pltpu.VMEM((3, 2, TOK, DROWS), F32),
            pltpu.VMEM((2, 4, TOK, DROWS), F32),
            pltpu.VMEM((8, 4, 16, TOK), BF16),
            pltpu.VMEM((4, 8, 16, TOK), BF16),
            pltpu.VMEM((8, 4, 16, DROWS), BF16),
            pltpu.VMEM((4, 8, 16, DROWS), BF16),
            pltpu.VMEM((4, DROWS, 128), BF16),
            pltpu.VMEM((RANK, HALF), F32),
            pltpu.VMEM((8, 16, COLS), F32),
            pltpu.VMEM((2, 4, 16, COLS), F32),
            pltpu.VMEM((8, 16, 128), F32),
            pltpu.VMEM((2, 4, 16, 128), F32),
            pltpu.VMEM((4, 4, 16, 128), F32),
            pltpu.VMEM((64, HALF), F32),
            pltpu.VMEM((2, 2, 16, HALF), F32),
            pltpu.VMEM((TOK, RANK), F32),
            pltpu.VMEM((ROWS, COLS), F32),
            pltpu.VMEM((ROWS, COLS), F32),
            pltpu.VMEM((ROWS, COLS), F32),
            dma((6,)),
            dma((1,)),
            dma((3, 2)),
            dma((6,)),
            dma((7, 3)),
            dma((2,)),
            dma((2, 4, 2)),
            dma((2,)),
            dma((2, 4, 2)),
            dma((2,)),
            dma((2, 4)),
            dma((2,)),
            dma((2, 4)),
            dma((1,)),
            dma((3,)),
            dma((8,)),
            dma((8,)),
            dma((8, 4)),
            dma((8, 4)),
            dma((3, 2)),
            dma((3, 2)),
            dma((2, 4)),
            dma((2, 4)),
        ],
        compiler_params=pltpu.CompilerParams(
            collective_id=0, has_side_effects=True, vmem_limit_bytes=56 * 1024 * 1024
        ),
    )(grad_out, weight, saved, first_moment, second_moment, basis, new_basis)
    return pl.pallas_call(
        hand_over,
        out_shape=(jax.ShapeDtypeStruct((TOK, RANK), F32), rank, rank, rank),
        in_specs=[hbm] * 4,
        out_specs=(hbm,) * 4,
        scratch_shapes=[pltpu.VMEM((TOK, RANK), F32)] + [pltpu.VMEM((ROWS, COLS), F32)] * 3 + [dma((2, 7))],
    )(*results)


def solution(mesh):
    return jax.shard_map(
        per_device,
        mesh=mesh,
        in_specs=(
            P("seq", "tp"),
            P("seq", "tp"),
            P("seq", None),
            P("seq", "tp"),
            P("seq", "tp"),
            P("seq", None),
            P("seq", None),
        ),
        out_specs=(P("seq", "tp"), P("seq", "tp"), P("seq", "tp"), P("seq", "tp")),
        check_vma=False,
    )
```
